32 devices in a mesh: tm: 8 (over z, y), chan: 4 (over x, core).
Axes of the slice: x: 2, y: 2, z: 4, core: 2. Of those that a mesh axis runs over, the one named last changes fastest.
Arguments:
- tokens: bfloat16 [16384, 1024], P('tm', 'chan'), may hold values from -170 to 170
- w_query: bfloat16 [1024, 1024], P(None, 'chan'), may hold values from -0.1875 to 0.1875
- w_key: bfloat16 [1024, 1024], P(None, 'chan'), may hold values from -0.1875 to 0.1875
- w_value: bfloat16 [1024, 1024], P(None, 'chan'), may hold values from -0.1875 to 0.1875
- w_out: bfloat16 [1024, 1024], P('chan'), may hold values from -0.25 to 0.25
- pool_kernel: float32 [2, 27, 64], replicated, may hold values from -1.25 to 1.25
Outputs:
- block_out: bfloat16 [16384, 1024], P('tm', 'chan')
The draws below stay inside these ranges and needn't reach their ends.
All inputs are finite; a program needn't handle non-finite values.
Results may differ from the reference program's by a relative error of at most 0.0053.
Values may be sent and summed in bfloat16 or wider, within the bound.
A program may use at most 128 MiB of HBM per device.

```python
import math
import jax
import jax.numpy as jnp
from jax import lax

D = 1024
HEADS = 16
HDIM = 64
HH = 16
WW = 16
TOK_DEV = 2048
POOLED = 64
FRAMES = 64
TOKENS = 16384
N_TM = 8


def draw_tokens(key, part):
    first_key = jax.random.fold_in(key, 0)
    normal_draw = jax.random.normal(first_key, (TOKENS, D), jnp.float32)
    return jnp.clip(normal_draw, -6.0, 6.0).astype(jnp.bfloat16)


def spiked(values, key, source, target, parts, factor):
    def block_of(position):
        return (jnp.arange(values.shape[position]) // (values.shape[position] // parts)).reshape((-1,) + (1,) * (values.ndim - 1 - position))

    first = jax.random.permutation(key, parts)[block_of(target)]
    second = (block_of(target) + parts // 2) % parts
    return jnp.where((block_of(source) == first) | (block_of(source) == second), factor * values, values)


def shard_levels(rng, shape, pieces, smallest, high):
    level, own = 1.0, jax.random.fold_in(rng, 6)
    for position, blocks in pieces:
        heights = jnp.exp(jax.random.uniform(jax.random.fold_in(own, position), (blocks,), jnp.float32, smallest / len(pieces), high / len(pieces)))
        level = level * jnp.repeat(heights, shape[position] // blocks).reshape([-1 if axis == position else 1 for axis in range(len(shape))])
    return level


def bell_draw(stream_key, shape, deviation, bound, shards=(), kind=jnp.bfloat16):
    result = jax.random.normal(stream_key, shape, jnp.float32) * deviation
    if len(shards) > 0:
        result = shard_levels(stream_key, shape, shards, -0.22, 0.18) * result
    return jnp.clip(result, min=-bound, max=bound).astype(kind)


def noise_with(key, extent, scale, most, shards, heavy, held_as=jnp.bfloat16):
    drawn = scale * jax.random.normal(key, extent, jnp.float32)
    if shards:
        drawn = drawn * shard_levels(key, extent, shards, -0.22, 0.18)
    return jnp.clip(spiked(drawn, jax.random.fold_in(key, 3), *heavy), -most, most).astype(held_as)


def setup_inputs(seed: int = 0) -> dict:
    key_of = jax.random.split(jax.random.key(seed), 7)
    return {
        "tokens": draw_tokens(jax.random.fold_in(key_of[6], 71), 0),
        "w_query": bell_draw(key_of[1], (D, D), D ** -0.5, 0.1875, ((1, 4),)),
        "w_key": bell_draw(key_of[2], (D, D), D ** -0.5, 0.1875, ((1, 4),)),
        "w_value": bell_draw(key_of[3], (D, D), D ** -0.5, 0.1875, ((1, 4),)),
        "w_out": noise_with(key_of[4], (D, D), D ** -0.5, 0.25, ((0, 4),), (0, 1, 4, 2.0)),
        "pool_kernel": bell_draw(key_of[5], (2, 27, HDIM), 27 ** -0.5, 1.25, (), jnp.float32),
    }


epsilon = 1e-06

def head_norm(field, head_width):
    shape = field.shape
    split = field.reshape(shape[:-1] + (shape[-1] // head_width, head_width))
    center = split - lax.optimization_barrier(jnp.mean(split, axis=-1, keepdims=True))
    spread = lax.optimization_barrier(jnp.mean(center * center, axis=-1, keepdims=True))
    return (center * lax.rsqrt(spread + epsilon)).reshape(shape)

def pool_field(field, kernel):
    earlier = jnp.roll(field, 1, axis=0)
    sources = (earlier[0::2], field[0::2], field[1::2])
    running = jnp.zeros((field.shape[0] // 2, HH // 4, WW // 4, field.shape[3]), jnp.float32)
    for first in range(3):
        padded = jnp.pad(sources[first], ((0, 0), (1, 0), (1, 0), (0, 0)))
        for second in range(3):
            for third in range(3):
                picked = padded[:, second:second + HH:4, third:third + WW:4, :]
                running = running + picked * kernel[9 * first + 3 * second + third]
    return running

def reference(tokens, w_query, w_key, w_value, w_out, pool_kernel):
    reach = min(6, (N_TM - 1) // 2)
    key_all = jnp.dot(tokens, w_key, preferred_element_type=jnp.float32).astype(jnp.bfloat16)
    value_all = jnp.dot(tokens, w_value, preferred_element_type=jnp.float32).astype(jnp.bfloat16)
    kernel_k = jnp.tile(pool_kernel[0], (1, HEADS))
    kernel_v = jnp.tile(pool_kernel[1], (1, HEADS))
    pooled_k = pool_field(key_all.astype(jnp.float32).reshape(FRAMES, HH, WW, D), kernel_k)
    pooled_k = head_norm(pooled_k, HDIM).astype(jnp.bfloat16).reshape(N_TM, POOLED, D)
    pooled_v = pool_field(value_all.astype(jnp.float32).reshape(FRAMES, HH, WW, D), kernel_v)
    pooled_v = head_norm(pooled_v, HDIM).astype(jnp.bfloat16).reshape(N_TM, POOLED, D)

    def one_block(index):
        rows_here = lax.dynamic_slice_in_dim(tokens, (index * TOK_DEV).astype(jnp.int32), TOK_DEV, 0)
        queries = jnp.dot(rows_here, w_query, preferred_element_type=jnp.float32).astype(jnp.bfloat16)
        chosen = (index + jnp.arange(-reach, reach + 1, dtype=jnp.int32)) % N_TM
        key_rows = pooled_k[chosen].reshape(-1, HEADS, HDIM).astype(jnp.float32)
        value_rows = pooled_v[chosen].reshape(-1, HEADS, HDIM).astype(jnp.float32)
        query_heads = queries.astype(jnp.float32).reshape(TOK_DEV, HEADS, HDIM)
        scores = jnp.einsum('qhd,khd->hqk', query_heads, key_rows) / math.sqrt(HDIM)
        highest = lax.optimization_barrier(jnp.max(scores, axis=-1, keepdims=True))
        weighted = jnp.exp(scores - highest)
        summed = lax.optimization_barrier(jnp.sum(weighted, axis=-1))
        weights_bf = weighted.astype(jnp.bfloat16).astype(jnp.float32)
        blended = jnp.einsum('hqk,khd->qhd', weights_bf, value_rows)
        attended = (blended / summed.T[:, :, None] + query_heads).astype(jnp.bfloat16).reshape(TOK_DEV, D)
        projected = jnp.dot(attended, w_out, preferred_element_type=jnp.float32)
        return (rows_here.astype(jnp.float32) + projected).astype(jnp.bfloat16)
    return lax.map(one_block, jnp.arange(N_TM, dtype=jnp.int32)).reshape(TOKENS, D)
```

```python
import functools

import jax
import jax.numpy as jnp
from jax import lax
from jax.experimental import pallas as pl
from jax.experimental.pallas import tpu as pltpu
from jax.sharding import PartitionSpec as P

D = 1024
HDIM = 64
HH = 16
WW = 16
FRAME = HH * WW
KEPT = 144
REST = FRAME - KEPT
CELLS = 16
CHUNK = 256
EPSILON = 1e-06
MESH = pl.DeviceIdType.MESH
HIGHEST = lax.Precision.HIGHEST
f32 = jnp.float32
bf16 = jnp.bfloat16


def position(token):
    row, column = token >> 4, token & 15
    b, e = (row + 1) & 3, (column + 1) & 3
    i = jnp.where(b == 0, (row >> 2) + 1, row >> 2) & 3
    j = jnp.where(e == 0, (column >> 2) + 1, column >> 2) & 3
    rest = jnp.where(
        b == 3, KEPT + (row >> 2) * 16 + column, KEPT + 64 + (b * 4 + i) * 4 + (column >> 2)
    )
    return jnp.where((b == 3) | (e == 3), rest, (3 * b + e) * 16 + i * 4 + j)


def kernel(
    n_tm, reach, frames, width,
    tokens, w_query, w_key, w_value, w_out, pool_hbm, out,
    pool_kernel, raw, tok_a, tok_b, w_kv, wq_own, wq_far, wo, place, place_back, taps, pre,
    halo_out, halo_in, gat, k_big, v_big, queries, resid, att, leaving,
    local_sem, a_send, a_recv, b_send, b_recv, wqx_send, wqx_recv, wq_send, wq_recv,
    wox_send, wox_recv, wo_send, wo_recv, halo_send, halo_recv, kvx_send, kvx_recv,
    gat_send, gat_recv, att_send, att_recv, out_send, out_recv,
):
    tm = lax.axis_index("tm")
    me = lax.axis_index("chan")
    sib = me + 1 - 2 * lax.rem(me, 2)
    across = lax.rem(me + 2, 4)
    diag = lax.rem(sib + 2, 4)
    heads = width // HDIM
    pairs = frames // 2
    half = frames // 2
    half_pairs = half // 2
    first = lax.div(me, 2) * half
    other_first = half - first
    relayed = n_tm == 8
    parts = n_tm if relayed else 1
    part = tm if relayed else 0
    beside = tm + 1 - 2 * lax.rem(tm, 2)
    offsets = [-2, -1, 1, 2, 4] if relayed else [d for d in range(-reach, reach + 1) if d != 0]

    def tm_at(d):
        return lax.rem(tm + d + n_tm, n_tm)

    def columns(chan):
        return pl.ds(pl.multiple_of(chan * width, width), width)

    pair_order = [pairs - 1] + list(range(pairs - 1))
    raw_loads = {
        p: pltpu.make_async_copy(
            tokens.at[pl.ds(2 * p, 2)], raw.at[pl.ds(2 * p, 2)], local_sem.at[8 + p]
        )
        for p in pair_order
    }
    for p in pair_order:
        raw_loads[p].start()
    loads = [
        pltpu.make_async_copy(w_key, w_kv.at[:, pl.ds(0, width)], local_sem.at[0]),
        pltpu.make_async_copy(w_value, w_kv.at[:, pl.ds(width, width)], local_sem.at[1]),
        pltpu.make_async_copy(pool_hbm, pool_kernel, local_sem.at[2]),
        pltpu.make_async_copy(w_query, wq_own, local_sem.at[3]),
        pltpu.make_async_copy(
            w_out.at[:, columns(me)], wo.at[0, :, pl.ds(0, width)], local_sem.at[4]
        ),
        pltpu.make_async_copy(
            w_out.at[:, columns(across)], wo.at[0, :, pl.ds(width, width)], local_sem.at[5]
        ),
    ]
    for load in loads:
        load.start()

    barrier = pltpu.get_barrier_semaphore()
    for other in (sib, across, diag):
        pl.semaphore_signal(barrier, inc=1, device_id={"chan": other}, device_id_type=MESH)
    for d in offsets:
        pl.semaphore_signal(barrier, inc=1, device_id={"tm": tm_at(d)}, device_id_type=MESH)

    line = lax.broadcasted_iota(jnp.int32, (1, FRAME), 1)
    spot = lax.broadcasted_iota(jnp.int32, (FRAME, FRAME), 0)
    place[...] = jnp.where(position(line) == spot, 1.0, 0.0).astype(bf16)
    pl.semaphore_wait(barrier, 3 + len(offsets))

    sent = []

    wq_rows = D // parts
    wo_rows = width // parts

    def wq_part(index):
        return wq_far.at[pl.ds(pl.multiple_of(index * wq_rows, wq_rows), wq_rows)]

    def wo_part(index):
        return wo.at[pl.ds(2, 2), pl.ds(pl.multiple_of(index * wo_rows, wo_rows), wo_rows)]

    wq_cross = pltpu.make_async_remote_copy(
        src_ref=w_query.at[pl.ds(pl.multiple_of(part * wq_rows, wq_rows), wq_rows)],
        dst_ref=wq_part(part), send_sem=wqx_send, recv_sem=wqx_recv,
        device_id={"chan": across}, device_id_type=MESH,
    )
    wq_cross.start()
    sent.append(wq_cross)

    def wo_copy(index, slot, other, block, chan):
        rows = (
            pl.ds(0, width)
            if slot == 1
            else pl.ds(pl.multiple_of(part * wo_rows, wo_rows), wo_rows)
        )
        return pltpu.make_async_remote_copy(
            src_ref=w_out.at[rows, columns(chan)],
            dst_ref=wo.at[slot, rows, pl.ds(block * width, width)],
            send_sem=wox_send.at[index], recv_sem=wox_recv.at[index],
            device_id={"chan": other}, device_id_type=MESH,
        )

    wo_far = [
        wo_copy(0, 2, across, 0, across),
        wo_copy(1, 2, across, 1, me),
        wo_copy(2, 3, diag, 0, diag),
        wo_copy(3, 3, diag, 1, sib),
    ]
    wo_near = [wo_copy(4, 1, sib, 0, sib), wo_copy(5, 1, sib, 1, diag)]

    def gather(part_of, send_at, recv_at):
        def copy(index, source, target):
            ref = part_of(source)
            return pltpu.make_async_remote_copy(
                src_ref=ref, dst_ref=ref, send_sem=send_at(index), recv_sem=recv_at(source),
                device_id={"tm": target}, device_id_type=MESH,
            )

        def own(targets):
            for index, target in enumerate(targets):
                one = copy(index, tm, target)
                one.start()
                sent.append(one)

        def relay():
            for index, d in enumerate((2, 6, 4)):
                one = copy(4 + index, tm_at(d), beside)
                one.wait_recv()
                one.start()
                sent.append(one)

        def arrived(slot):
            copy(0, slot, beside).wait_recv()

        return own, relay, arrived

    wq_own_go, wq_relay, wq_arrived = gather(
        wq_part, lambda i: wq_send.at[i], lambda s: wq_recv.at[s]
    )
    wo_own_go, wo_relay, wo_arrived = gather(
        wo_part, lambda i: wo_send.at[i], lambda s: wo_recv.at[s]
    )
    plane = [tm_at(2), tm_at(6), tm_at(4), beside]
    from_beside = [beside] + [lax.rem(beside + d, n_tm) for d in (2, 6, 4)]

    def a_ref(slot, p):
        return tok_a.at[slot, pl.ds(2 * p, 2)]

    def b_ref(slot, base, p):
        return tok_b.at[slot, pl.ds(base + 2 * p, 2)]

    def chan_copy(ref, send, recv, other):
        return pltpu.make_async_remote_copy(
            src_ref=ref, dst_ref=ref, send_sem=send, recv_sem=recv,
            device_id={"chan": other}, device_id_type=MESH,
        )

    def a_copy(kind, p):
        slot = (me, me, across)[kind]
        return chan_copy(a_ref(slot, p), a_send.at[kind, p], a_recv.at[kind, p], (across, sib, sib)[kind])

    def a_arrival(kind, p):
        slot = (across, sib, diag)[kind]
        return chan_copy(a_ref(slot, p), a_send.at[kind, p], a_recv.at[kind, p], (across, sib, sib)[kind])

    def b_copy(kind, p):
        slot = (me, me, across)[kind]
        base = other_first if kind == 0 else first
        return chan_copy(
            b_ref(slot, base, p), b_send.at[kind, p], b_recv.at[kind, p], (across, sib, sib)[kind]
        )

    def b_arrival(kind, p):
        slot = (across, sib, diag)[kind]
        return chan_copy(
            b_ref(slot, first, p), b_send.at[kind, p], b_recv.at[kind, p], (across, sib, sib)[kind]
        )

    def go(copy):
        copy.start()
        sent.append(copy)

    for p in pair_order:
        raw_loads[p].wait()
        for frame in (2 * p, 2 * p + 1):
            moved = jnp.dot(place[...], raw[frame], preferred_element_type=f32).astype(bf16)
            tok_a[me, frame] = moved[:KEPT]
            tok_b[me, frame] = moved[KEPT:]
        go(a_copy(0, p))
        go(a_copy(1, p))
        if p == pair_order[0]:
            for copy in wo_far:
                go(copy)
    for copy in wo_near:
        go(copy)
    for p in range(half_pairs):
        go(b_copy(1, p))

    loads[2].wait()
    channel = lax.broadcasted_iota(jnp.int32, (HDIM, 2 * width), 1)
    inner = lax.broadcasted_iota(jnp.int32, (HDIM, 2 * width), 0)
    same = lax.rem(channel, HDIM) == inner
    spread_k = (same & (channel < width)).astype(f32)
    spread_v = (same & (channel >= width)).astype(f32)
    wide = jnp.dot(pool_kernel[:, 0], spread_k, precision=HIGHEST, preferred_element_type=f32)
    wide = wide + jnp.dot(pool_kernel[:, 1], spread_v, precision=HIGHEST, preferred_element_type=f32)
    cell = lax.broadcasted_iota(jnp.int32, (CELLS, 2 * width), 0)
    for tap in range(27):
        b, e = tap % 9 // 3, tap % 3
        value = jnp.broadcast_to(wide[tap : tap + 1], (CELLS, 2 * width))
        if b == 0:
            value = jnp.where(cell < 4, 0.0, value)
        if e == 0:
            value = jnp.where((cell & 3) == 0, 0.0, value)
        taps[tap] = value
    pre[...] = jnp.zeros_like(pre)
    line = lax.broadcasted_iota(jnp.int32, (FRAME, FRAME), 1)
    spot = lax.broadcasted_iota(jnp.int32, (FRAME, 1), 0)
    place_back[...] = jnp.where(position(spot) == line, 1.0, 0.0).astype(bf16)

    wq_cross.wait_recv()
    if relayed:
        wq_own_go(plane)

    halo = pltpu.make_async_remote_copy(
        src_ref=halo_out, dst_ref=halo_in, send_sem=halo_send, recv_sem=halo_recv,
        device_id={"tm": tm_at(1)}, device_id_type=MESH,
    )

    for load in loads[:2]:
        load.wait()

    def project(p):
        a_arrival(0, p).wait_recv()
        go(a_copy(2, p))
        a_arrival(1, p).wait_recv()
        a_arrival(2, p).wait_recv()
        total = None
        for s in range(4):
            term = jnp.dot(
                tok_a[s, 2 * p : 2 * p + 2].reshape(2 * KEPT, width),
                w_kv[s * width : (s + 1) * width, :],
                preferred_element_type=f32,
            )
            total = term if total is None else total + term
        field = total.astype(bf16).astype(f32)
        here, later = pre[p], None
        for tap in range(9):
            even = field[tap * CELLS : (tap + 1) * CELLS]
            odd = field[KEPT + tap * CELLS : KEPT + (tap + 1) * CELLS]
            here = here + even * taps[9 + tap] + odd * taps[18 + tap]
            ahead = odd * taps[tap]
            later = ahead if later is None else later + ahead
        pre[p] = here
        if p == pairs - 1:
            halo_out[...] = later
            go(halo)
        else:
            pre[p + 1] = pre[p + 1] + later

    g0 = lax.broadcasted_iota(jnp.int32, (width, width), 0) // HDIM
    g1 = lax.broadcasted_iota(jnp.int32, (width, width), 1) // HDIM
    averaging = jnp.where(g0 == g1, 1.0 / HDIM, 0.0).astype(bf16)
    phase_rows = half_pairs * CELLS

    def head_mean(x, pieces):
        stack, rest = [], x
        for _ in range(pieces):
            piece = rest.astype(bf16)
            stack.append(piece)
            rest = rest - piece.astype(f32)
        means = jnp.dot(jnp.concatenate(stack, axis=0), averaging, preferred_element_type=f32)
        total = None
        for index in reversed(range(pieces)):
            term = means[index * x.shape[0] : (index + 1) * x.shape[0]]
            total = term if total is None else total + term
        return total

    def normalise(phase):
        pooled = pre[phase * half_pairs : (phase + 1) * half_pairs].reshape(phase_rows, 2 * width)
        if phase == 0:
            pooled = jnp.concatenate([pooled[:CELLS] + halo_in[...], pooled[CELLS:]], axis=0)
        x = jnp.concatenate([pooled[:, :width], pooled[:, width:]], axis=0)
        center = x - head_mean(x, 3)
        spread = head_mean(center * center, 2)
        result = (center * lax.rsqrt(spread + EPSILON)).astype(bf16)
        gat[0, tm, phase, :, :width] = result[:phase_rows]
        gat[0, tm, phase, :, width:] = result[phase_rows:]

    kv_gathers = {
        (g, phase): gather(
            lambda s, g=g, phase=phase: gat.at[g, s, phase],
            lambda i, g=g, phase=phase: gat_send.at[g, phase, i],
            lambda s, g=g, phase=phase: gat_recv.at[g, phase, s],
        )
        for g in range(2)
        for phase in range(2)
    }

    def kv_cross(phase):
        return pltpu.make_async_remote_copy(
            src_ref=gat.at[0, tm, phase], dst_ref=gat.at[1, tm, phase],
            send_sem=kvx_send.at[phase], recv_sem=kvx_recv.at[phase],
            device_id={"chan": across}, device_id_type=MESH,
        )

    kv_targets = plane if relayed else [tm_at(d) for d in offsets]

    def kv_send(phase):
        go(kv_cross(phase))
        kv_gathers[0, phase][0](kv_targets)

    def kv_forward(phase):
        kv_cross(phase).wait_recv()
        kv_gathers[1, phase][0](kv_targets)

    def kv_relay(g, phase):
        if relayed:
            kv_gathers[g, phase][1]()

    lane_head = lax.broadcasted_iota(jnp.int32, (phase_rows, width), 1) // HDIM

    def spread_block(g, where, slot, phase):
        start = (2 * where + phase) * phase_rows
        rows = slice(start, start + phase_rows)
        keys = gat[g, slot, phase, :, :width]
        values = gat[g, slot, phase, :, width:]
        for h in range(heads):
            k_big[g * heads + h, rows, :] = keys * jnp.where(lane_head == h, HDIM**-0.5, 0.0).astype(bf16)
            v_big[g * heads + h, rows, :] = values * jnp.where(lane_head == h, 1.0, 0.0).astype(bf16)

    def spread_blocks(g, phase):
        spread_block(g, 0, tm, phase)
        if relayed:
            for where, d in enumerate((2, 6)):
                spread_block(g, 1 + where, tm_at(d), phase)
            others, start = from_beside, 3
        else:
            others, start = [tm_at(d) for d in offsets], 1
        for where, slot in enumerate(others):
            kv_gathers[g, phase][2](slot)
            spread_block(g, start + where, slot, phase)

    project(pair_order[0])
    if relayed:
        wq_relay()
    for copy in wo_far:
        copy.wait_recv()
    if relayed:
        wo_own_go(plane)
    project(pair_order[1])
    if relayed:
        wo_relay()
    project(pair_order[2])
    for p in range(half_pairs // 2):
        go(b_copy(0, p))
    halo.wait_recv()
    normalise(0)
    kv_send(0)
    kv_forward(0)
    kv_relay(0, 0)
    project(pair_order[3])
    normalise(1)
    kv_send(1)
    for p in range(half_pairs // 2, half_pairs):
        go(b_copy(0, p))
    kv_relay(1, 0)
    kv_forward(1)
    spread_blocks(0, 0)
    kv_relay(0, 1)
    spread_blocks(1, 0)
    kv_relay(1, 1)

    loads[3].wait()
    if relayed:
        for slot in from_beside:
            wq_arrived(slot)
    for p in range(half_pairs):
        b_arrival(0, p).wait_recv()
        go(b_copy(2, p))
    for p in range(half_pairs):
        b_arrival(1, p).wait_recv()
        b_arrival(2, p).wait_recv()
        for local in (2 * p, 2 * p + 1):
            frame = first + local
            rows = slice(local * FRAME, (local + 1) * FRAME)
            near, far = None, None
            for s in range(4):
                block = jnp.concatenate([tok_a[s, frame], tok_b[s, frame]], axis=0)
                depth = slice(s * width, (s + 1) * width)
                near_term = jnp.dot(block, wq_own[depth], preferred_element_type=f32)
                far_term = jnp.dot(block, wq_far[depth], preferred_element_type=f32)
                near = near_term if near is None else near + near_term
                far = far_term if far is None else far + far_term
            back = place_back[...]
            queries[0, rows] = jnp.dot(back, near.astype(bf16), preferred_element_type=f32).astype(bf16)
            queries[1, rows] = jnp.dot(back, far.astype(bf16), preferred_element_type=f32).astype(bf16)
            block = jnp.concatenate([tok_a[across, frame], tok_b[across, frame]], axis=0)
            resid[rows] = jnp.dot(back, block, preferred_element_type=f32).astype(bf16)

    spread_blocks(0, 1)
    spread_blocks(1, 1)

    for copy in wo_near:
        copy.wait_recv()
    for load in loads[4:]:
        load.wait()
    if relayed:
        for slot in from_beside:
            wo_arrived(slot)

    out_head = lax.broadcasted_iota(jnp.int32, (CHUNK, width), 1) // HDIM
    chunks = half * FRAME // CHUNK

    def rows_of(chunk):
        return pl.ds(pl.multiple_of(chunk * CHUNK, CHUNK), CHUNK)

    def att_copy(g, chunk):
        return pltpu.make_async_remote_copy(
            src_ref=att.at[2 * g, rows_of(chunk)], dst_ref=att.at[2 * g + 1, rows_of(chunk)],
            send_sem=att_send.at[g, chunk], recv_sem=att_recv.at[g, chunk],
            device_id={"chan": sib}, device_id_type=MESH,
        )

    def out_rows(base, chunk):
        return pl.ds(pl.multiple_of(base * FRAME + chunk * CHUNK, CHUNK), CHUNK)

    def out_copy(chunk, base):
        return pltpu.make_async_remote_copy(
            src_ref=leaving.at[rows_of(chunk)], dst_ref=out.at[out_rows(base, chunk)],
            send_sem=out_send.at[chunk], recv_sem=out_recv.at[chunk],
            device_id={"chan": across}, device_id_type=MESH,
        )

    def attend(chunk):
        rows = rows_of(chunk)
        for g in range(2):
            q = queries[g, rows]
            blended = None
            divisor = None
            for h in range(heads):
                scores = lax.dot_general(
                    q, k_big[g * heads + h], (((1,), (1,)), ((), ())), preferred_element_type=f32
                )
                weighted = jnp.exp(scores - jnp.max(scores, axis=-1, keepdims=True))
                summed = jnp.sum(weighted, axis=-1, keepdims=True)
                term = jnp.dot(
                    weighted.astype(bf16), v_big[g * heads + h], preferred_element_type=f32
                )
                blended = term if blended is None else blended + term
                wide_sum = jnp.broadcast_to(summed, (CHUNK, width))
                divisor = wide_sum if divisor is None else jnp.where(out_head == h, wide_sum, divisor)
            att[2 * g, rows] = (blended / divisor + q.astype(f32)).astype(bf16)
            att_copy(g, chunk).start()

    def finish(chunk):
        rows = rows_of(chunk)
        for g in range(2):
            att_copy(g, chunk).wait_recv()
        total = None
        for s in (0, 2, 1, 3):
            term = jnp.dot(att[s, rows], wo[s], preferred_element_type=f32)
            total = term if total is None else total + term
        leaving[rows] = (total[:, width:] + resid[rows].astype(f32)).astype(bf16)
        out_copy(chunk, first).start()
        per_frame = FRAME // CHUNK
        frame = first + lax.div(chunk, per_frame)
        inside = pl.ds(pl.multiple_of(lax.rem(chunk, per_frame) * CHUNK, CHUNK), CHUNK)
        out[out_rows(first, chunk)] = (total[:, :width] + raw[frame, inside].astype(f32)).astype(bf16)

    attend(0)

    @pl.loop(1, chunks)
    def _(chunk):
        attend(chunk)
        finish(chunk - 1)

    finish(chunks - 1)

    @pl.loop(0, chunks)
    def _(chunk):
        for g in range(2):
            att_copy(g, chunk).wait_send()
        out_copy(chunk, other_first).wait_recv()
        out_copy(chunk, first).wait_send()

    for copy in sent:
        copy.wait_send()


def per_device(n_tm, n_chan, tokens, w_query, w_key, w_value, w_out, pool_kernel):
    rows, width = tokens.shape
    frames = rows // FRAME
    pairs = frames // 2
    half = frames // 2
    half_pairs = half // 2
    chunks = half * FRAME // CHUNK
    reach = min(6, (n_tm - 1) // 2)
    spans = 2 * reach + 1
    heads = width // HDIM
    block = pairs * CELLS
    dma = pltpu.SemaphoreType.DMA
    anywhere = pl.BlockSpec(memory_space=pltpu.HBM)
    vmem = pl.BlockSpec(memory_space=pltpu.VMEM)
    return pl.pallas_call(
        functools.partial(kernel, n_tm, reach, frames, width),
        out_shape=jax.ShapeDtypeStruct((rows, width), bf16),
        in_specs=[anywhere] * 6,
        out_specs=vmem,
        scratch_shapes=[
            pltpu.VMEM((27, 2, HDIM), f32),
            pltpu.VMEM((frames, FRAME, width), bf16),
            pltpu.VMEM((n_chan, frames, KEPT, width), bf16),
            pltpu.VMEM((n_chan, frames, REST, width), bf16),
            pltpu.VMEM((D, 2 * width), bf16),
            pltpu.VMEM((D, width), bf16),
            pltpu.VMEM((D, width), bf16),
            pltpu.VMEM((n_chan, width, 2 * width), bf16),
            pltpu.VMEM((FRAME, FRAME), bf16),
            pltpu.VMEM((FRAME, FRAME), bf16),
            pltpu.VMEM((27, CELLS, 2 * width), f32),
            pltpu.VMEM((pairs, CELLS, 2 * width), f32),
            pltpu.VMEM((CELLS, 2 * width), f32),
            pltpu.VMEM((CELLS, 2 * width), f32),
            pltpu.VMEM((2, n_tm, 2, block // 2, 2 * width), bf16),
            pltpu.VMEM((2 * heads, spans * block, width), bf16),
            pltpu.VMEM((2 * heads, spans * block, width), bf16),
            pltpu.VMEM((2, half * FRAME, width), bf16),
            pltpu.VMEM((half * FRAME, width), bf16),
            pltpu.VMEM((n_chan, half * FRAME, width), bf16),
            pltpu.VMEM((half * FRAME, width), bf16),
            dma((8 + pairs,)),
            dma((3, pairs)),
            dma((3, pairs)),
            dma((3, half_pairs)),
            dma((3, half_pairs)),
            dma,
            dma,
            dma((7,)),
            dma((n_tm,)),
            dma((6,)),
            dma((6,)),
            dma((7,)),
            dma((n_tm,)),
            dma,
            dma,
            dma((2,)),
            dma((2,)),
            dma((2, 2, max(7, 2 * reach))),
            dma((2, 2, n_tm)),
            dma((2, chunks)),
            dma((2, chunks)),
            dma((chunks,)),
            dma((chunks,)),
        ],
        compiler_params=pltpu.CompilerParams(
            collective_id=0, has_side_effects=True, vmem_limit_bytes=63 * 1024 * 1024
        ),
    )(
        tokens.reshape(frames, FRAME, width), w_query, w_key, w_value, w_out,
        pool_kernel.transpose(1, 0, 2),
    )


def solution(mesh):
    shape = dict(mesh.shape)
    return jax.shard_map(
        functools.partial(per_device, shape["tm"], shape["chan"]),
        mesh=mesh,
        in_specs=(
            P("tm", "chan"),
            P(None, "chan"),
            P(None, "chan"),
            P(None, "chan"),
            P("chan", None),
            P(),
        ),
        out_specs=P("tm", "chan"),
        check_vma=False,
    )
```

```python
import functools

import jax
import jax.numpy as jnp
from jax import lax
from jax.experimental import pallas as pl
from jax.experimental.pallas import tpu as pltpu
from jax.sharding import PartitionSpec as P

D = 1024
HDIM = 64
HH = 16
WW = 16
FRAME = HH * WW
KEPT = 144
REST = FRAME - KEPT
CELLS = 16
CHUNK = 128
VMEM_LIMIT = 251 * 256 * 1024
EPSILON = 1e-06
MESH = pl.DeviceIdType.MESH
HIGHEST = lax.Precision.HIGHEST
f32 = jnp.float32
bf16 = jnp.bfloat16


def position(token):
    row, column = token >> 4, token & 15
    b, e = (row + 1) & 3, (column + 1) & 3
    i = jnp.where(b == 0, (row >> 2) + 1, row >> 2) & 3
    j = jnp.where(e == 0, (column >> 2) + 1, column >> 2) & 3
    rest = jnp.where(
        b == 3, KEPT + (row >> 2) * 16 + column, KEPT + 64 + (b * 4 + i) * 4 + (column >> 2)
    )
    return jnp.where((b == 3) | (e == 3), rest, (3 * b + e) * 16 + i * 4 + j)


def kernel(
    n_tm, reach, frames, width,
    tokens, w_query, w_key, w_value, w_out, pool_hbm, out,
    pool_kernel, raw, tok_a, tok_b, w_kv, wq_own, wq_far, wo, place, place_back, taps, pre,
    halo_out, halo_in, gat, k_big, v_big, queries, resid, early, att, leaving,
    local_sem, a_send, a_recv, b_send, b_recv, wqx_send, wqx_recv, wq_send, wq_recv,
    wox_send, wox_recv, wo_send, wo_recv, halo_send, halo_recv, kvx_send, kvx_recv,
    gat_send, gat_recv, att_send, att_recv, out_send, out_recv,
):
    tm = lax.axis_index("tm")
    me = lax.axis_index("chan")
    sib = me + 1 - 2 * lax.rem(me, 2)
    across = lax.rem(me + 2, 4)
    diag = lax.rem(sib + 2, 4)
    heads = width // HDIM
    spans = 2 * reach + 1
    pairs = frames // 2
    half = frames // 2
    half_pairs = half // 2
    first = lax.div(me, 2) * half
    other_first = half - first
    relayed = n_tm == 8
    parts = n_tm if relayed else 1
    part = tm if relayed else 0
    beside = tm + 1 - 2 * lax.rem(tm, 2)
    offsets = [-2, -1, 1, 2, 4] if relayed else [d for d in range(-reach, reach + 1) if d != 0]

    def tm_at(d):
        return lax.rem(tm + d + n_tm, n_tm)

    def columns(chan):
        return pl.ds(pl.multiple_of(chan * width, width), width)

    pair_order = [pairs - 1] + list(range(pairs - 1))
    raw_loads = {
        p: pltpu.make_async_copy(
            tokens.at[pl.ds(2 * p, 2)], raw.at[pl.ds(2 * p, 2)], local_sem.at[8 + p]
        )
        for p in pair_order
    }
    for p in pair_order:
        raw_loads[p].start()
    loads = [
        pltpu.make_async_copy(w_key, w_kv.at[:, pl.ds(0, width)], local_sem.at[0]),
        pltpu.make_async_copy(w_value, w_kv.at[:, pl.ds(width, width)], local_sem.at[1]),
        pltpu.make_async_copy(pool_hbm, pool_kernel, local_sem.at[2]),
        pltpu.make_async_copy(w_query, wq_own, local_sem.at[3]),
        pltpu.make_async_copy(
            w_out.at[:, columns(me)], wo.at[0, :, pl.ds(0, width)], local_sem.at[4]
        ),
        pltpu.make_async_copy(
            w_out.at[:, columns(across)], wo.at[0, :, pl.ds(width, width)], local_sem.at[5]
        ),
    ]
    for load in loads:
        load.start()

    barrier = pltpu.get_barrier_semaphore()
    for other in (sib, across, diag):
        pl.semaphore_signal(barrier, inc=1, device_id={"chan": other}, device_id_type=MESH)
    for d in offsets:
        pl.semaphore_signal(barrier, inc=1, device_id={"tm": tm_at(d)}, device_id_type=MESH)

    line = lax.broadcasted_iota(jnp.int32, (1, FRAME), 1)
    spot = lax.broadcasted_iota(jnp.int32, (FRAME, FRAME), 0)
    place[...] = jnp.where(position(line) == spot, 1.0, 0.0).astype(bf16)
    pl.semaphore_wait(barrier, 3 + len(offsets))

    sent = []

    def go(copy):
        copy.start()
        sent.append(copy)

    wq_rows = D // parts
    wo_parts = 2 if relayed else 1
    wo_part_at = lax.rem(tm, 2) if relayed else 0
    wo_rows = width // wo_parts

    def wq_part(index):
        return wq_far.at[pl.ds(pl.multiple_of(index * wq_rows, wq_rows), wq_rows)]

    def wo_half(slot, index):
        return wo.at[slot, pl.ds(pl.multiple_of(index * wo_rows, wo_rows), wo_rows)]

    wq_cross = pltpu.make_async_remote_copy(
        src_ref=w_query.at[pl.ds(pl.multiple_of(part * wq_rows, wq_rows), wq_rows)],
        dst_ref=wq_part(part), send_sem=wqx_send, recv_sem=wqx_recv,
        device_id={"chan": across}, device_id_type=MESH,
    )
    wq_cross.start()
    sent.append(wq_cross)

    def wo_copy(index, slot, other, block, chan):
        rows = (
            pl.ds(0, width)
            if slot == 1
            else pl.ds(pl.multiple_of(wo_part_at * wo_rows, wo_rows), wo_rows)
        )
        return pltpu.make_async_remote_copy(
            src_ref=w_out.at[rows, columns(chan)],
            dst_ref=wo.at[slot, rows, pl.ds(block * width, width)],
            send_sem=wox_send.at[index], recv_sem=wox_recv.at[index],
            device_id={"chan": other}, device_id_type=MESH,
        )

    wo_far = [
        wo_copy(0, 2, across, 0, across),
        wo_copy(1, 2, across, 1, me),
        wo_copy(2, 3, diag, 0, diag),
        wo_copy(3, 3, diag, 1, sib),
    ]
    wo_near = [wo_copy(4, 1, sib, 0, sib), wo_copy(5, 1, sib, 1, diag)]

    def gather(part_of, send_at, recv_at):
        def copy(index, source, target):
            ref = part_of(source)
            return pltpu.make_async_remote_copy(
                src_ref=ref, dst_ref=ref, send_sem=send_at(index), recv_sem=recv_at(source),
                device_id={"tm": target}, device_id_type=MESH,
            )

        def own(targets):
            for index, target in enumerate(targets):
                one = copy(index, tm, target)
                one.start()
                sent.append(one)

        def relay():
            for index, d in enumerate((2, 6, 4)):
                one = copy(4 + index, tm_at(d), beside)
                one.wait_recv()
                one.start()
                sent.append(one)

        def arrived(slot):
            copy(0, slot, beside).wait_recv()

        return own, relay, arrived

    wq_own_go, wq_relay, wq_arrived = gather(
        wq_part, lambda i: wq_send.at[i], lambda s: wq_recv.at[s]
    )

    def wo_swap(slot, index):
        ref = wo_half(slot, index)
        return pltpu.make_async_remote_copy(
            src_ref=ref, dst_ref=ref, send_sem=wo_send.at[slot - 2], recv_sem=wo_recv.at[slot - 2],
            device_id={"tm": beside}, device_id_type=MESH,
        )

    def wo_forward(slot):
        for copy in wo_far[2 * (slot - 2) : 2 * (slot - 1)]:
            copy.wait_recv()
        if relayed:
            go(wo_swap(slot, wo_part_at))

    plane = [tm_at(2), tm_at(6), tm_at(4), beside]
    from_beside = [beside] + [lax.rem(beside + d, n_tm) for d in (2, 6, 4)]

    def a_ref(slot, p):
        return tok_a.at[slot, pl.ds(2 * p, 2)]

    def b_ref(slot, base, p):
        return tok_b.at[slot, pl.ds(base + 2 * p, 2)]

    def chan_copy(ref, send, recv, other):
        return pltpu.make_async_remote_copy(
            src_ref=ref, dst_ref=ref, send_sem=send, recv_sem=recv,
            device_id={"chan": other}, device_id_type=MESH,
        )

    def a_copy(kind, p):
        slot = (me, me, across)[kind]
        return chan_copy(a_ref(slot, p), a_send.at[kind, p], a_recv.at[kind, p], (across, sib, sib)[kind])

    def a_arrival(kind, p):
        slot = (across, sib, diag)[kind]
        return chan_copy(a_ref(slot, p), a_send.at[kind, p], a_recv.at[kind, p], (across, sib, sib)[kind])

    def b_copy(kind, p):
        slot = (me, me, across)[kind]
        base = other_first if kind == 0 else first
        return chan_copy(
            b_ref(slot, base, p), b_send.at[kind, p], b_recv.at[kind, p], (across, sib, sib)[kind]
        )

    def b_arrival(kind, p):
        slot = (across, sib, diag)[kind]
        return chan_copy(
            b_ref(slot, first, p), b_send.at[kind, p], b_recv.at[kind, p], (across, sib, sib)[kind]
        )

    for p in pair_order:
        raw_loads[p].wait()
        for frame in (2 * p, 2 * p + 1):
            moved = jnp.dot(place[...], raw[frame], preferred_element_type=f32).astype(bf16)
            tok_a[me, frame] = moved[:KEPT]
            tok_b[me, frame] = moved[KEPT:]
        go(a_copy(0, p))
        go(a_copy(1, p))
    for copy in wo_near:
        go(copy)
    for p in range(half_pairs):
        go(b_copy(1, p))

    loads[2].wait()
    channel = lax.broadcasted_iota(jnp.int32, (HDIM, 2 * width), 1)
    inner = lax.broadcasted_iota(jnp.int32, (HDIM, 2 * width), 0)
    same = lax.rem(channel, HDIM) == inner
    spread_k = (same & (channel < width)).astype(f32)
    spread_v = (same & (channel >= width)).astype(f32)
    wide = jnp.dot(pool_kernel[:, 0], spread_k, precision=HIGHEST, preferred_element_type=f32)
    wide = wide + jnp.dot(pool_kernel[:, 1], spread_v, precision=HIGHEST, preferred_element_type=f32)
    cell = lax.broadcasted_iota(jnp.int32, (CELLS, 2 * width), 0)
    for tap in range(27):
        b, e = tap % 9 // 3, tap % 3
        value = jnp.broadcast_to(wide[tap : tap + 1], (CELLS, 2 * width))
        if b == 0:
            value = jnp.where(cell < 4, 0.0, value)
        if e == 0:
            value = jnp.where((cell & 3) == 0, 0.0, value)
        taps[tap] = value
    pre[...] = jnp.zeros_like(pre)
    line = lax.broadcasted_iota(jnp.int32, (FRAME, FRAME), 1)
    spot = lax.broadcasted_iota(jnp.int32, (FRAME, 1), 0)
    place_back[...] = jnp.where(position(spot) == line, 1.0, 0.0).astype(bf16)

    wq_cross.wait_recv()
    if relayed:
        wq_own_go(plane)

    halo = pltpu.make_async_remote_copy(
        src_ref=halo_out, dst_ref=halo_in, send_sem=halo_send, recv_sem=halo_recv,
        device_id={"tm": tm_at(1)}, device_id_type=MESH,
    )

    for load in loads[:2]:
        load.wait()

    def project(p, meanwhile=()):
        a_arrival(0, p).wait_recv()
        go(a_copy(2, p))
        for step in meanwhile:
            step()
        a_arrival(1, p).wait_recv()
        a_arrival(2, p).wait_recv()
        total = None
        for s in range(4):
            term = jnp.dot(
                tok_a[s, 2 * p : 2 * p + 2].reshape(2 * KEPT, width),
                w_kv[s * width : (s + 1) * width, :],
                preferred_element_type=f32,
            )
            total = term if total is None else total + term
        field = total.astype(bf16).astype(f32)
        here, later = pre[p], None
        for tap in range(9):
            even = field[tap * CELLS : (tap + 1) * CELLS]
            odd = field[KEPT + tap * CELLS : KEPT + (tap + 1) * CELLS]
            here = here + even * taps[9 + tap] + odd * taps[18 + tap]
            ahead = odd * taps[tap]
            later = ahead if later is None else later + ahead
        pre[p] = here
        if p == pairs - 1:
            halo_out[...] = later
            go(halo)
        else:
            pre[p + 1] = pre[p + 1] + later

    g0 = lax.broadcasted_iota(jnp.int32, (width, width), 0) // HDIM
    g1 = lax.broadcasted_iota(jnp.int32, (width, width), 1) // HDIM
    averaging = jnp.where(g0 == g1, 1.0 / HDIM, 0.0).astype(bf16)
    phases = [(p, 1) for p in range(half_pairs)] + [(half_pairs, half_pairs)]

    def head_mean(x, pieces):
        stack, rest = [], x
        for _ in range(pieces):
            piece = rest.astype(bf16)
            stack.append(piece)
            rest = rest - piece.astype(f32)
        means = jnp.dot(jnp.concatenate(stack, axis=0), averaging, preferred_element_type=f32)
        total = None
        for index in reversed(range(pieces)):
            term = means[index * x.shape[0] : (index + 1) * x.shape[0]]
            total = term if total is None else total + term
        return total

    def normalise(phase):
        start, count = phases[phase]
        rows = count * CELLS
        pooled = pre[start : start + count].reshape(rows, 2 * width)
        if phase == 0:
            pooled = pooled + halo_in[...]
        x = jnp.concatenate([pooled[:, :width], pooled[:, width:]], axis=0)
        center = x - head_mean(x, 3)
        spread = head_mean(center * center, 2)
        result = (center * lax.rsqrt(spread + EPSILON)).astype(bf16)
        ours = gat.at[0, tm, pl.ds(start, count)]
        ours[:, :, :width] = result[:rows].reshape(count, CELLS, width)
        ours[:, :, width:] = result[rows:].reshape(count, CELLS, width)

    def block(g, slot, phase):
        return gat.at[g, slot, pl.ds(*phases[phase])]

    kv_gathers = {
        (g, phase): gather(
            lambda s, g=g, phase=phase: block(g, s, phase),
            lambda i, g=g, phase=phase: gat_send.at[g, phase, i],
            lambda s, g=g, phase=phase: gat_recv.at[g, phase, s],
        )
        for g in range(2)
        for phase in range(len(phases))
    }

    def kv_cross(phase):
        return pltpu.make_async_remote_copy(
            src_ref=block(0, tm, phase), dst_ref=block(1, tm, phase),
            send_sem=kvx_send.at[phase], recv_sem=kvx_recv.at[phase],
            device_id={"chan": across}, device_id_type=MESH,
        )

    kv_targets = plane if relayed else [tm_at(d) for d in offsets]

    def kv_send(phase):
        go(kv_cross(phase))
        kv_gathers[0, phase][0](kv_targets)

    def kv_forward(phase):
        kv_cross(phase).wait_recv()
        kv_gathers[1, phase][0](kv_targets)

    def kv_relay(g, phase):
        if relayed:
            kv_gathers[g, phase][1]()

    lane_head = lax.broadcasted_iota(jnp.int32, (CELLS, width), 1) // HDIM

    def spread_block(g, where, slot, phase):
        start, count = phases[phase]
        for pooled in range(start, start + count):
            at = (pooled * spans + where) * CELLS
            keys = gat[g, slot, pooled, :, :width]
            values = gat[g, slot, pooled, :, width:]
            for h in range(heads):
                k_big[g * heads + h, at : at + CELLS, :] = keys * jnp.where(
                    lane_head == h, HDIM**-0.5, 0.0
                ).astype(bf16)
                v_big[g * heads + h, at : at + CELLS, :] = values * jnp.where(
                    lane_head == h, 1.0, 0.0
                ).astype(bf16)

    def spread_blocks(g, phase):
        spread_block(g, 0, tm, phase)
        if relayed:
            for where, d in enumerate((2, 6)):
                spread_block(g, 1 + where, tm_at(d), phase)
            others, start = from_beside, 3
        else:
            others, start = [tm_at(d) for d in offsets], 1
        for where, slot in enumerate(others):
            kv_gathers[g, phase][2](slot)
            spread_block(g, start + where, slot, phase)

    def query_start(p):
        b_arrival(0, p).wait_recv()
        go(b_copy(2, p))

    def query(p):
        b_arrival(1, p).wait_recv()
        b_arrival(2, p).wait_recv()
        for local in (2 * p, 2 * p + 1):
            frame = first + local
            rows = slice(local * FRAME, (local + 1) * FRAME)
            near, far = None, None
            for s in range(4):
                block = jnp.concatenate([tok_a[s, frame], tok_b[s, frame]], axis=0)
                depth = slice(s * width, (s + 1) * width)
                near_term = jnp.dot(block, wq_own[depth], preferred_element_type=f32)
                far_term = jnp.dot(block, wq_far[depth], preferred_element_type=f32)
                near = near_term if near is None else near + near_term
                far = far_term if far is None else far + far_term
            back = place_back[...]
            queries[0, rows] = jnp.dot(back, near.astype(bf16), preferred_element_type=f32).astype(bf16)
            queries[1, rows] = jnp.dot(back, far.astype(bf16), preferred_element_type=f32).astype(bf16)
            block = jnp.concatenate([tok_a[across, frame], tok_b[across, frame]], axis=0)
            resid[rows] = jnp.dot(back, block, preferred_element_type=f32).astype(bf16)

    out_head = lax.broadcasted_iota(jnp.int32, (CHUNK, width), 1) // HDIM
    per_pair = 2 * FRAME // CHUNK
    phase_keys = spans * half_pairs * CELLS
    chunks = half * FRAME // CHUNK

    def rows_of(chunk):
        return pl.ds(pl.multiple_of(chunk * CHUNK, CHUNK), CHUNK)

    def att_copy(g, chunk):
        return pltpu.make_async_remote_copy(
            src_ref=att.at[2 * g, rows_of(chunk)], dst_ref=att.at[2 * g + 1, rows_of(chunk)],
            send_sem=att_send.at[g, chunk], recv_sem=att_recv.at[g, chunk],
            device_id={"chan": sib}, device_id_type=MESH,
        )

    def out_rows(base, chunk):
        return pl.ds(pl.multiple_of(base * FRAME + chunk * CHUNK, CHUNK), CHUNK)

    def out_copy(chunk, base):
        return pltpu.make_async_remote_copy(
            src_ref=leaving.at[rows_of(chunk)], dst_ref=out.at[out_rows(base, chunk)],
            send_sem=out_send.at[chunk], recv_sem=out_recv.at[chunk],
            device_id={"chan": across}, device_id_type=MESH,
        )

    def attend(chunk, g, phase):
        q = queries[g, rows_of(chunk)]
        keys = slice(phase * phase_keys, (phase + 1) * phase_keys)
        blended = top = divisor = None
        for h in range(heads):
            scores = lax.dot_general(
                q, k_big[g * heads + h, keys], (((1,), (1,)), ((), ())), preferred_element_type=f32
            )
            highest = jnp.max(scores, axis=-1, keepdims=True)
            weighted = jnp.exp(scores - highest)
            summed = jnp.sum(weighted, axis=-1, keepdims=True)
            term = jnp.dot(
                weighted.astype(bf16), v_big[g * heads + h, keys], preferred_element_type=f32
            )
            blended = term if blended is None else blended + term
            wide_top = jnp.broadcast_to(highest, (CHUNK, width))
            wide_sum = jnp.broadcast_to(summed, (CHUNK, width))
            top = wide_top if top is None else jnp.where(out_head == h, wide_top, top)
            divisor = wide_sum if divisor is None else jnp.where(out_head == h, wide_sum, divisor)
        return blended, top, divisor

    def attend_early(g, p):
        @pl.loop(p * per_pair, (p + 1) * per_pair)
        def _(chunk):
            rows = rows_of(chunk)
            early[0, g, rows], early[1, g, rows], early[2, g, rows] = attend(chunk, g, 0)

    def attend_late(chunk):
        rows = rows_of(chunk)
        for g in range(2):
            blended, top, divisor = attend(chunk, g, 1)
            old_top = early[1, g, rows]
            new_top = jnp.maximum(top, old_top)
            keep, add = jnp.exp(old_top - new_top), jnp.exp(top - new_top)
            blended = early[0, g, rows] * keep + blended * add
            divisor = early[2, g, rows] * keep + divisor * add
            att[2 * g, rows] = (blended / divisor + queries[g, rows].astype(f32)).astype(bf16)
            att_copy(g, chunk).start()

    def finish(chunk):
        rows = rows_of(chunk)
        for g in range(2):
            att_copy(g, chunk).wait_recv()
        total = None
        for s in (0, 2, 1, 3):
            term = jnp.dot(att[s, rows], wo[s], preferred_element_type=f32)
            total = term if total is None else total + term
        leaving[rows] = (total[:, width:] + resid[rows].astype(f32)).astype(bf16)
        out_copy(chunk, first).start()
        per_frame = FRAME // CHUNK
        frame = first + lax.div(chunk, per_frame)
        inside = pl.ds(pl.multiple_of(lax.rem(chunk, per_frame) * CHUNK, CHUNK), CHUNK)
        out[out_rows(first, chunk)] = (total[:, :width] + raw[frame, inside].astype(f32)).astype(bf16)

    last = len(phases) - 1
    project(pair_order[0])
    project(pair_order[1])
    halo.wait_recv()
    normalise(0)
    kv_send(0)
    if relayed:
        wq_relay()
    project(pair_order[2])
    normalise(1)
    kv_send(1)
    go(b_copy(0, 0))
    kv_relay(0, 0)
    project(pair_order[3], [lambda: kv_forward(0), lambda: kv_forward(1)])
    normalise(2)
    kv_send(2)
    for copy in wo_far[:2]:
        go(copy)
    go(b_copy(0, 1))
    for copy in wo_far[2:]:
        go(copy)
    kv_relay(0, 1)
    query_start(0)
    kv_forward(2)
    kv_relay(1, 0)
    kv_relay(1, 1)
    loads[3].wait()
    if relayed:
        for slot in from_beside:
            wq_arrived(slot)
    query(0)
    spread_blocks(0, 0)
    spread_blocks(0, 1)
    kv_relay(0, 2)
    kv_relay(1, 2)
    attend_early(0, 0)
    wo_forward(2)
    query_start(1)
    spread_blocks(1, 0)
    spread_blocks(1, 1)
    attend_early(1, 0)
    query(1)
    wo_forward(3)
    attend_early(0, 1)
    attend_early(1, 1)
    spread_blocks(0, 2)
    spread_blocks(1, 2)
    for copy in wo_near:
        copy.wait_recv()
    for load in loads[4:]:
        load.wait()
    if relayed:
        for slot in (2, 3):
            wo_swap(slot, 1 - wo_part_at).wait_recv()

    attend_late(0)

    @pl.loop(1, chunks)
    def _(chunk):
        attend_late(chunk)
        finish(chunk - 1)

    finish(chunks - 1)

    @pl.loop(0, chunks)
    def _(chunk):
        for g in range(2):
            att_copy(g, chunk).wait_send()
        out_copy(chunk, other_first).wait_recv()
        out_copy(chunk, first).wait_send()

    for copy in sent:
        copy.wait_send()


def per_device(n_tm, n_chan, tokens, w_query, w_key, w_value, w_out, pool_kernel):
    rows, width = tokens.shape
    frames = rows // FRAME
    pairs = frames // 2
    half = frames // 2
    half_pairs = half // 2
    chunks = half * FRAME // CHUNK
    reach = min(6, (n_tm - 1) // 2)
    spans = 2 * reach + 1
    heads = width // HDIM
    block = pairs * CELLS
    dma = pltpu.SemaphoreType.DMA
    anywhere = pl.BlockSpec(memory_space=pltpu.HBM)
    vmem = pl.BlockSpec(memory_space=pltpu.VMEM)
    return pl.pallas_call(
        functools.partial(kernel, n_tm, reach, frames, width),
        out_shape=pltpu.VMEM((rows, width), bf16),
        in_specs=[anywhere] * 6,
        out_specs=vmem,
        scratch_shapes=[
            pltpu.VMEM((27, 2, HDIM), f32),
            pltpu.VMEM((frames, FRAME, width), bf16),
            pltpu.VMEM((n_chan, frames, KEPT, width), bf16),
            pltpu.VMEM((n_chan, frames, REST, width), bf16),
            pltpu.VMEM((D, 2 * width), bf16),
            pltpu.VMEM((D, width), bf16),
            pltpu.VMEM((D, width), bf16),
            pltpu.VMEM((n_chan, width, 2 * width), bf16),
            pltpu.VMEM((FRAME, FRAME), bf16),
            pltpu.VMEM((FRAME, FRAME), bf16),
            pltpu.VMEM((27, CELLS, 2 * width), f32),
            pltpu.VMEM((pairs, CELLS, 2 * width), f32),
            pltpu.VMEM((CELLS, 2 * width), f32),
            pltpu.VMEM((CELLS, 2 * width), f32),
            pltpu.VMEM((2, n_tm, pairs, CELLS, 2 * width), bf16),
            pltpu.VMEM((2 * heads, spans * block, width), bf16),
            pltpu.VMEM((2 * heads, spans * block, width), bf16),
            pltpu.VMEM((2, half * FRAME, width), bf16),
            pltpu.VMEM((half * FRAME, width), bf16),
            pltpu.VMEM((3, 2, half * FRAME, width), f32),
            pltpu.VMEM((n_chan, half * FRAME, width), bf16),
            pltpu.VMEM((half * FRAME, width), bf16),
            dma((8 + pairs,)),
            dma((3, pairs)),
            dma((3, pairs)),
            dma((3, half_pairs)),
            dma((3, half_pairs)),
            dma,
            dma,
            dma((7,)),
            dma((n_tm,)),
            dma((6,)),
            dma((6,)),
            dma((2,)),
            dma((2,)),
            dma,
            dma,
            dma((3,)),
            dma((3,)),
            dma((2, 3, max(7, 2 * reach))),
            dma((2, 3, n_tm)),
            dma((2, chunks)),
            dma((2, chunks)),
            dma((chunks,)),
            dma((chunks,)),
        ],
        compiler_params=pltpu.CompilerParams(
            collective_id=0, has_side_effects=True, vmem_limit_bytes=VMEM_LIMIT
        ),
    )(
        tokens.reshape(frames, FRAME, width), w_query, w_key, w_value, w_out,
        pool_kernel.transpose(1, 0, 2),
    )


def solution(mesh):
    shape = dict(mesh.shape)
    return jax.shard_map(
        functools.partial(per_device, shape["tm"], shape["chan"]),
        mesh=mesh,
        in_specs=(
            P("tm", "chan"),
            P(None, "chan"),
            P(None, "chan"),
            P(None, "chan"),
            P("chan", None),
            P(),
        ),
        out_specs=P("tm", "chan"),
        check_vma=False,
    )
```

```python
import functools

import jax
import jax.numpy as jnp
from jax import lax
from jax.experimental import pallas as pl
from jax.experimental.pallas import tpu as pltpu
from jax.sharding import PartitionSpec as P

D = 1024
HDIM = 64
HH = 16
WW = 16
FRAME = HH * WW
KEPT = 144
REST = FRAME - KEPT
CELLS = 16
CHUNK = 128
VMEM_LIMIT = 251 * 256 * 1024
EPSILON = 1e-06
MESH = pl.DeviceIdType.MESH
HIGHEST = lax.Precision.HIGHEST
f32 = jnp.float32
bf16 = jnp.bfloat16


def position(token):
    row, column = token >> 4, token & 15
    b, e = (row + 1) & 3, (column + 1) & 3
    i = jnp.where(b == 0, (row >> 2) + 1, row >> 2) & 3
    j = jnp.where(e == 0, (column >> 2) + 1, column >> 2) & 3
    rest = jnp.where(
        b == 3, KEPT + (row >> 2) * 16 + column, KEPT + 64 + (b * 4 + i) * 4 + (column >> 2)
    )
    return jnp.where((b == 3) | (e == 3), rest, (3 * b + e) * 16 + i * 4 + j)


def kernel(
    n_tm, reach, frames, width,
    tokens, w_query, w_key, w_value, w_out, pool_hbm, out,
    pool_kernel, raw, tok_a, tok_b, w_kv, wq_own, wq_far, wo, place, place_back, taps, pre,
    halo_out, halo_in, gat, k_big, v_big, queries, resid, early, att, leaving,
    local_sem, a_send, a_recv, b_send, b_recv, wqx_send, wqx_recv, wq_send, wq_recv,
    wox_send, wox_recv, wo_send, wo_recv, halo_send, halo_recv, kvx_send, kvx_recv,
    gat_send, gat_recv, att_send, att_recv, out_send, out_recv,
):
    tm = lax.axis_index("tm")
    me = lax.axis_index("chan")
    sib = me + 1 - 2 * lax.rem(me, 2)
    across = lax.rem(me + 2, 4)
    diag = lax.rem(sib + 2, 4)
    heads = width // HDIM
    spans = 2 * reach + 1
    pairs = frames // 2
    half = frames // 2
    half_pairs = half // 2
    first = lax.div(me, 2) * half
    other_first = half - first
    relayed = n_tm == 8
    parts = n_tm if relayed else 1
    part = tm if relayed else 0
    beside = tm + 1 - 2 * lax.rem(tm, 2)
    offsets = [-2, -1, 1, 2, 4] if relayed else [d for d in range(-reach, reach + 1) if d != 0]

    def tm_at(d):
        return lax.rem(tm + d + n_tm, n_tm)

    def columns(chan):
        return pl.ds(pl.multiple_of(chan * width, width), width)

    pair_order = [pairs - 1] + list(range(pairs - 1))
    raw_loads = {
        p: pltpu.make_async_copy(
            tokens.at[pl.ds(2 * p, 2)], raw.at[pl.ds(2 * p, 2)], local_sem.at[8 + p]
        )
        for p in pair_order
    }
    for p in pair_order:
        raw_loads[p].start()
    loads = [
        pltpu.make_async_copy(w_key, w_kv.at[:, pl.ds(0, width)], local_sem.at[0]),
        pltpu.make_async_copy(w_value, w_kv.at[:, pl.ds(width, width)], local_sem.at[1]),
        pltpu.make_async_copy(pool_hbm, pool_kernel, local_sem.at[2]),
        pltpu.make_async_copy(w_query, wq_own, local_sem.at[3]),
        pltpu.make_async_copy(
            w_out.at[:, columns(me)], wo.at[0, :, pl.ds(0, width)], local_sem.at[4]
        ),
        pltpu.make_async_copy(
            w_out.at[:, columns(across)], wo.at[0, :, pl.ds(width, width)], local_sem.at[5]
        ),
    ]
    for load in loads:
        load.start()

    barrier = pltpu.get_barrier_semaphore()
    for other in (sib, across, diag):
        pl.semaphore_signal(barrier, inc=1, device_id={"chan": other}, device_id_type=MESH)
    for d in offsets:
        pl.semaphore_signal(barrier, inc=1, device_id={"tm": tm_at(d)}, device_id_type=MESH)

    line = lax.broadcasted_iota(jnp.int32, (1, FRAME), 1)
    spot = lax.broadcasted_iota(jnp.int32, (FRAME, FRAME), 0)
    place[...] = jnp.where(position(line) == spot, 1.0, 0.0).astype(bf16)
    pl.semaphore_wait(barrier, 3 + len(offsets))

    sent = []

    def go(copy):
        copy.start()
        sent.append(copy)

    wq_rows = D // parts
    wo_parts = 2 if relayed else 1
    wo_part_at = lax.rem(tm, 2) if relayed else 0
    wo_rows = width // wo_parts

    def wq_part(index):
        return wq_far.at[pl.ds(pl.multiple_of(index * wq_rows, wq_rows), wq_rows)]

    def wo_half(slot, index):
        return wo.at[slot, pl.ds(pl.multiple_of(index * wo_rows, wo_rows), wo_rows)]

    wq_cross = pltpu.make_async_remote_copy(
        src_ref=w_query.at[pl.ds(pl.multiple_of(part * wq_rows, wq_rows), wq_rows)],
        dst_ref=wq_part(part), send_sem=wqx_send, recv_sem=wqx_recv,
        device_id={"chan": across}, device_id_type=MESH,
    )
    wq_cross.start()
    sent.append(wq_cross)

    def wo_copy(index, slot, other, block, chan):
        rows = (
            pl.ds(0, width)
            if slot == 1
            else pl.ds(pl.multiple_of(wo_part_at * wo_rows, wo_rows), wo_rows)
        )
        return pltpu.make_async_remote_copy(
            src_ref=w_out.at[rows, columns(chan)],
            dst_ref=wo.at[slot, rows, pl.ds(block * width, width)],
            send_sem=wox_send.at[index], recv_sem=wox_recv.at[index],
            device_id={"chan": other}, device_id_type=MESH,
        )

    wo_far = [
        wo_copy(0, 2, across, 0, across),
        wo_copy(1, 2, across, 1, me),
        wo_copy(2, 3, diag, 0, diag),
        wo_copy(3, 3, diag, 1, sib),
    ]
    wo_near = [wo_copy(4, 1, sib, 0, sib), wo_copy(5, 1, sib, 1, diag)]

    def gather(part_of, send_at, recv_at):
        def copy(index, source, target):
            ref = part_of(source)
            return pltpu.make_async_remote_copy(
                src_ref=ref, dst_ref=ref, send_sem=send_at(index), recv_sem=recv_at(source),
                device_id={"tm": target}, device_id_type=MESH,
            )

        def own(targets):
            for index, target in enumerate(targets):
                one = copy(index, tm, target)
                one.start()
                sent.append(one)

        def relay():
            for index, d in enumerate((2, 6, 4)):
                one = copy(4 + index, tm_at(d), beside)
                one.wait_recv()
                one.start()
                sent.append(one)

        def arrived(slot):
            copy(0, slot, beside).wait_recv()

        return own, relay, arrived

    wq_own_go, wq_relay, wq_arrived = gather(
        wq_part, lambda i: wq_send.at[i], lambda s: wq_recv.at[s]
    )

    def wo_swap(slot, index):
        ref = wo_half(slot, index)
        return pltpu.make_async_remote_copy(
            src_ref=ref, dst_ref=ref, send_sem=wo_send.at[slot - 2], recv_sem=wo_recv.at[slot - 2],
            device_id={"tm": beside}, device_id_type=MESH,
        )

    def wo_forward(slot):
        for copy in wo_far[2 * (slot - 2) : 2 * (slot - 1)]:
            copy.wait_recv()
        if relayed:
            go(wo_swap(slot, wo_part_at))

    plane = [tm_at(2), tm_at(6), tm_at(4), beside]
    from_beside = [beside] + [lax.rem(beside + d, n_tm) for d in (2, 6, 4)]

    def a_ref(slot, p):
        return tok_a.at[slot, pl.ds(2 * p, 2)]

    def b_ref(slot, base, p):
        return tok_b.at[slot, pl.ds(base + 2 * p, 2)]

    def chan_copy(ref, send, recv, other):
        return pltpu.make_async_remote_copy(
            src_ref=ref, dst_ref=ref, send_sem=send, recv_sem=recv,
            device_id={"chan": other}, device_id_type=MESH,
        )

    def a_copy(kind, p):
        slot = (me, me, across)[kind]
        return chan_copy(a_ref(slot, p), a_send.at[kind, p], a_recv.at[kind, p], (across, sib, sib)[kind])

    def a_arrival(kind, p):
        slot = (across, sib, diag)[kind]
        return chan_copy(a_ref(slot, p), a_send.at[kind, p], a_recv.at[kind, p], (across, sib, sib)[kind])

    def b_copy(kind, p):
        slot = (me, me, across)[kind]
        base = other_first if kind == 0 else first
        return chan_copy(
            b_ref(slot, base, p), b_send.at[kind, p], b_recv.at[kind, p], (across, sib, sib)[kind]
        )

    def b_arrival(kind, p):
        slot = (across, sib, diag)[kind]
        return chan_copy(
            b_ref(slot, first, p), b_send.at[kind, p], b_recv.at[kind, p], (across, sib, sib)[kind]
        )

    for p in pair_order:
        raw_loads[p].wait()
        for frame in (2 * p, 2 * p + 1):
            moved = jnp.dot(place[...], raw[frame], preferred_element_type=f32).astype(bf16)
            tok_a[me, frame] = moved[:KEPT]
            tok_b[me, frame] = moved[KEPT:]
        go(a_copy(0, p))
        go(a_copy(1, p))
    for copy in wo_near:
        go(copy)
    for p in range(half_pairs):
        go(b_copy(1, p))

    loads[2].wait()
    channel = lax.broadcasted_iota(jnp.int32, (HDIM, 2 * width), 1)
    inner = lax.broadcasted_iota(jnp.int32, (HDIM, 2 * width), 0)
    same = lax.rem(channel, HDIM) == inner
    spread_k = (same & (channel < width)).astype(f32)
    spread_v = (same & (channel >= width)).astype(f32)
    wide = jnp.dot(pool_kernel[:, 0], spread_k, precision=HIGHEST, preferred_element_type=f32)
    wide = wide + jnp.dot(pool_kernel[:, 1], spread_v, precision=HIGHEST, preferred_element_type=f32)
    cell = lax.broadcasted_iota(jnp.int32, (CELLS, 2 * width), 0)
    for tap in range(27):
        b, e = tap % 9 // 3, tap % 3
        value = jnp.broadcast_to(wide[tap : tap + 1], (CELLS, 2 * width))
        if b == 0:
            value = jnp.where(cell < 4, 0.0, value)
        if e == 0:
            value = jnp.where((cell & 3) == 0, 0.0, value)
        taps[tap] = value
    pre[...] = jnp.zeros_like(pre)
    line = lax.broadcasted_iota(jnp.int32, (FRAME, FRAME), 1)
    spot = lax.broadcasted_iota(jnp.int32, (FRAME, 1), 0)
    place_back[...] = jnp.where(position(spot) == line, 1.0, 0.0).astype(bf16)

    wq_cross.wait_recv()
    if relayed:
        wq_own_go(plane)

    halo = pltpu.make_async_remote_copy(
        src_ref=halo_out, dst_ref=halo_in, send_sem=halo_send, recv_sem=halo_recv,
        device_id={"tm": tm_at(1)}, device_id_type=MESH,
    )

    for load in loads[:2]:
        load.wait()

    def project(p, meanwhile=()):
        a_arrival(0, p).wait_recv()
        go(a_copy(2, p))
        for step in meanwhile:
            step()
        a_arrival(1, p).wait_recv()
        a_arrival(2, p).wait_recv()
        total = None
        for s in range(4):
            term = jnp.dot(
                tok_a[s, 2 * p : 2 * p + 2].reshape(2 * KEPT, width),
                w_kv[s * width : (s + 1) * width, :],
                preferred_element_type=f32,
            )
            total = term if total is None else total + term
        field = total.astype(bf16).astype(f32)
        here, later = pre[p], None
        for tap in range(9):
            even = field[tap * CELLS : (tap + 1) * CELLS]
            odd = field[KEPT + tap * CELLS : KEPT + (tap + 1) * CELLS]
            here = here + even * taps[9 + tap] + odd * taps[18 + tap]
            ahead = odd * taps[tap]
            later = ahead if later is None else later + ahead
        pre[p] = here
        if p == pairs - 1:
            halo_out[...] = later
            go(halo)
        else:
            pre[p + 1] = pre[p + 1] + later

    g0 = lax.broadcasted_iota(jnp.int32, (width, width), 0) // HDIM
    g1 = lax.broadcasted_iota(jnp.int32, (width, width), 1) // HDIM
    averaging = jnp.where(g0 == g1, 1.0 / HDIM, 0.0).astype(bf16)
    phases = [(p, 1) for p in range(half_pairs)] + [(half_pairs, half_pairs)]

    def head_mean(x, pieces):
        stack, rest = [], x
        for _ in range(pieces):
            piece = rest.astype(bf16)
            stack.append(piece)
            rest = rest - piece.astype(f32)
        means = jnp.dot(jnp.concatenate(stack, axis=0), averaging, preferred_element_type=f32)
        total = None
        for index in reversed(range(pieces)):
            term = means[index * x.shape[0] : (index + 1) * x.shape[0]]
            total = term if total is None else total + term
        return total

    def normalise(phase):
        start, count = phases[phase]
        rows = count * CELLS
        pooled = pre[start : start + count].reshape(rows, 2 * width)
        if phase == 0:
            pooled = pooled + halo_in[...]
        x = jnp.concatenate([pooled[:, :width], pooled[:, width:]], axis=0)
        center = x - head_mean(x, 3)
        spread = head_mean(center * center, 2)
        result = (center * lax.rsqrt(spread + EPSILON)).astype(bf16)
        ours = gat.at[0, tm, pl.ds(start, count)]
        ours[:, :, :width] = result[:rows].reshape(count, CELLS, width)
        ours[:, :, width:] = result[rows:].reshape(count, CELLS, width)

    def block(g, slot, phase):
        return gat.at[g, slot, pl.ds(*phases[phase])]

    kv_gathers = {
        (g, phase): gather(
            lambda s, g=g, phase=phase: block(g, s, phase),
            lambda i, g=g, phase=phase: gat_send.at[g, phase, i],
            lambda s, g=g, phase=phase: gat_recv.at[g, phase, s],
        )
        for g in range(2)
        for phase in range(len(phases))
    }

    def kv_cross(phase):
        return pltpu.make_async_remote_copy(
            src_ref=block(0, tm, phase), dst_ref=block(1, tm, phase),
            send_sem=kvx_send.at[phase], recv_sem=kvx_recv.at[phase],
            device_id={"chan": across}, device_id_type=MESH,
        )

    kv_targets = plane if relayed else [tm_at(d) for d in offsets]

    def kv_send(phase):
        go(kv_cross(phase))
        kv_gathers[0, phase][0](kv_targets)

    def kv_forward(phase):
        kv_cross(phase).wait_recv()
        kv_gathers[1, phase][0](kv_targets)

    def kv_relay(g, phase):
        if relayed:
            kv_gathers[g, phase][1]()

    lane_head = lax.broadcasted_iota(jnp.int32, (CELLS, width), 1) // HDIM

    def spread_block(g, where, slot, phase):
        start, count = phases[phase]
        for pooled in range(start, start + count):
            at = (pooled * spans + where) * CELLS
            keys = gat[g, slot, pooled, :, :width]
            values = gat[g, slot, pooled, :, width:]
            for h in range(heads):
                k_big[g * heads + h, at : at + CELLS, :] = keys * jnp.where(
                    lane_head == h, HDIM**-0.5, 0.0
                ).astype(bf16)
                v_big[g * heads + h, at : at + CELLS, :] = values * jnp.where(
                    lane_head == h, 1.0, 0.0
                ).astype(bf16)

    def spread_blocks(g, phase):
        spread_block(g, 0, tm, phase)
        if relayed:
            for where, d in enumerate((2, 6)):
                spread_block(g, 1 + where, tm_at(d), phase)
            others, start = from_beside, 3
        else:
            others, start = [tm_at(d) for d in offsets], 1
        for where, slot in enumerate(others):
            kv_gathers[g, phase][2](slot)
            spread_block(g, start + where, slot, phase)

    def query_start(p):
        b_arrival(0, p).wait_recv()
        go(b_copy(2, p))

    def query(p):
        b_arrival(1, p).wait_recv()
        b_arrival(2, p).wait_recv()
        for local in (2 * p, 2 * p + 1):
            frame = first + local
            rows = slice(local * FRAME, (local + 1) * FRAME)
            near, far = None, None
            for s in range(4):
                block = jnp.concatenate([tok_a[s, frame], tok_b[s, frame]], axis=0)
                depth = slice(s * width, (s + 1) * width)
                near_term = jnp.dot(block, wq_own[depth], preferred_element_type=f32)
                far_term = jnp.dot(block, wq_far[depth], preferred_element_type=f32)
                near = near_term if near is None else near + near_term
                far = far_term if far is None else far + far_term
            back = place_back[...]
            queries[0, rows] = jnp.dot(back, near.astype(bf16), preferred_element_type=f32).astype(bf16)
            queries[1, rows] = jnp.dot(back, far.astype(bf16), preferred_element_type=f32).astype(bf16)
            block = jnp.concatenate([tok_a[across, frame], tok_b[across, frame]], axis=0)
            resid[rows] = jnp.dot(back, block, preferred_element_type=f32).astype(bf16)

    per_pair = 2 * FRAME // CHUNK
    phase_keys = spans * half_pairs * CELLS
    chunks = half * FRAME // CHUNK

    def rows_of(chunk):
        return pl.ds(pl.multiple_of(chunk * CHUNK, CHUNK), CHUNK)

    def att_copy(g, chunk):
        return pltpu.make_async_remote_copy(
            src_ref=att.at[2 * g, rows_of(chunk)], dst_ref=att.at[2 * g + 1, rows_of(chunk)],
            send_sem=att_send.at[g, chunk], recv_sem=att_recv.at[g, chunk],
            device_id={"chan": sib}, device_id_type=MESH,
        )

    def out_rows(base, chunk):
        return pl.ds(pl.multiple_of(base * FRAME + chunk * CHUNK, CHUNK), CHUNK)

    def out_copy(chunk, base):
        return pltpu.make_async_remote_copy(
            src_ref=leaving.at[rows_of(chunk)], dst_ref=out.at[out_rows(base, chunk)],
            send_sem=out_send.at[chunk], recv_sem=out_recv.at[chunk],
            device_id={"chan": across}, device_id_type=MESH,
        )

    def attend(rows, size, g, phase):
        q = queries[g, rows]
        head_of = lax.broadcasted_iota(jnp.int32, (size, width), 1) // HDIM
        keys = slice(phase * phase_keys, (phase + 1) * phase_keys)
        blended = top = divisor = None
        for h in range(heads):
            scores = lax.dot_general(
                q, k_big[g * heads + h, keys], (((1,), (1,)), ((), ())), preferred_element_type=f32
            )
            highest = jnp.max(scores, axis=-1, keepdims=True)
            weighted = jnp.exp(scores - highest)
            summed = jnp.sum(weighted, axis=-1, keepdims=True)
            term = jnp.dot(
                weighted.astype(bf16), v_big[g * heads + h, keys], preferred_element_type=f32
            )
            blended = term if blended is None else blended + term
            wide_top = jnp.broadcast_to(highest, (size, width))
            wide_sum = jnp.broadcast_to(summed, (size, width))
            top = wide_top if top is None else jnp.where(head_of == h, wide_top, top)
            divisor = wide_sum if divisor is None else jnp.where(head_of == h, wide_sum, divisor)
        return blended, top, divisor

    def attend_early(g, p):
        @pl.loop(2 * p, 2 * p + 2)
        def _(frame):
            rows = pl.ds(pl.multiple_of(frame * FRAME, FRAME), FRAME)
            early[0, g, rows], early[1, g, rows], early[2, g, rows] = attend(rows, FRAME, g, 0)

    def attend_late(chunk):
        rows = rows_of(chunk)
        for g in range(2):
            blended, top, divisor = attend(rows, CHUNK, g, 1)
            old_top = early[1, g, rows]
            new_top = jnp.maximum(top, old_top)
            keep, add = jnp.exp(old_top - new_top), jnp.exp(top - new_top)
            blended = early[0, g, rows] * keep + blended * add
            divisor = early[2, g, rows] * keep + divisor * add
            att[2 * g, rows] = (blended / divisor + queries[g, rows].astype(f32)).astype(bf16)
            att_copy(g, chunk).start()

    def finish(chunk):
        rows = rows_of(chunk)
        for g in range(2):
            att_copy(g, chunk).wait_recv()
        total = None
        for s in (0, 2, 1, 3):
            term = jnp.dot(att[s, rows], wo[s], preferred_element_type=f32)
            total = term if total is None else total + term
        leaving[rows] = (total[:, width:] + resid[rows].astype(f32)).astype(bf16)
        out_copy(chunk, first).start()
        per_frame = FRAME // CHUNK
        frame = first + lax.div(chunk, per_frame)
        inside = pl.ds(pl.multiple_of(lax.rem(chunk, per_frame) * CHUNK, CHUNK), CHUNK)
        out[out_rows(first, chunk)] = (total[:, :width] + raw[frame, inside].astype(f32)).astype(bf16)

    last = len(phases) - 1
    project(pair_order[0])
    project(pair_order[1])
    halo.wait_recv()
    normalise(0)
    kv_send(0)
    if relayed:
        wq_relay()
    project(pair_order[2])
    normalise(1)
    kv_send(1)
    go(b_copy(0, 0))
    kv_relay(0, 0)
    project(pair_order[3], [lambda: kv_forward(0), lambda: kv_forward(1)])
    normalise(2)
    kv_send(2)
    go(b_copy(0, 1))
    for copy in wo_far:
        go(copy)
    kv_relay(0, 1)
    query_start(0)
    kv_forward(2)
    kv_relay(1, 0)
    kv_relay(1, 1)
    loads[3].wait()
    if relayed:
        for slot in from_beside:
            wq_arrived(slot)
    query(0)
    spread_blocks(0, 0)
    spread_blocks(0, 1)
    kv_relay(0, 2)
    kv_relay(1, 2)
    attend_early(0, 0)
    wo_forward(2)
    query_start(1)
    spread_blocks(1, 0)
    spread_blocks(1, 1)
    attend_early(1, 0)
    query(1)
    wo_forward(3)
    attend_early(0, 1)
    attend_early(1, 1)
    spread_blocks(0, 2)
    spread_blocks(1, 2)
    for copy in wo_near:
        copy.wait_recv()
    for load in loads[4:]:
        load.wait()
    if relayed:
        for slot in (2, 3):
            wo_swap(slot, 1 - wo_part_at).wait_recv()

    attend_late(0)

    @pl.loop(1, chunks)
    def _(chunk):
        attend_late(chunk)
        finish(chunk - 1)

    finish(chunks - 1)

    @pl.loop(0, chunks)
    def _(chunk):
        for g in range(2):
            att_copy(g, chunk).wait_send()
        out_copy(chunk, other_first).wait_recv()
        out_copy(chunk, first).wait_send()

    for copy in sent:
        copy.wait_send()


def per_device(n_tm, n_chan, tokens, w_query, w_key, w_value, w_out, pool_kernel):
    rows, width = tokens.shape
    frames = rows // FRAME
    pairs = frames // 2
    half = frames // 2
    half_pairs = half // 2
    chunks = half * FRAME // CHUNK
    reach = min(6, (n_tm - 1) // 2)
    spans = 2 * reach + 1
    heads = width // HDIM
    block = pairs * CELLS
    dma = pltpu.SemaphoreType.DMA
    anywhere = pl.BlockSpec(memory_space=pltpu.HBM)
    vmem = pl.BlockSpec(memory_space=pltpu.VMEM)
    return pl.pallas_call(
        functools.partial(kernel, n_tm, reach, frames, width),
        out_shape=pltpu.VMEM((rows, width), bf16),
        in_specs=[anywhere] * 6,
        out_specs=vmem,
        scratch_shapes=[
            pltpu.VMEM((27, 2, HDIM), f32),
            pltpu.VMEM((frames, FRAME, width), bf16),
            pltpu.VMEM((n_chan, frames, KEPT, width), bf16),
            pltpu.VMEM((n_chan, frames, REST, width), bf16),
            pltpu.VMEM((D, 2 * width), bf16),
            pltpu.VMEM((D, width), bf16),
            pltpu.VMEM((D, width), bf16),
            pltpu.VMEM((n_chan, width, 2 * width), bf16),
            pltpu.VMEM((FRAME, FRAME), bf16),
            pltpu.VMEM((FRAME, FRAME), bf16),
            pltpu.VMEM((27, CELLS, 2 * width), f32),
            pltpu.VMEM((pairs, CELLS, 2 * width), f32),
            pltpu.VMEM((CELLS, 2 * width), f32),
            pltpu.VMEM((CELLS, 2 * width), f32),
            pltpu.VMEM((2, n_tm, pairs, CELLS, 2 * width), bf16),
            pltpu.VMEM((2 * heads, spans * block, width), bf16),
            pltpu.VMEM((2 * heads, spans * block, width), bf16),
            pltpu.VMEM((2, half * FRAME, width), bf16),
            pltpu.VMEM((half * FRAME, width), bf16),
            pltpu.VMEM((3, 2, half * FRAME, width), f32),
            pltpu.VMEM((n_chan, half * FRAME, width), bf16),
            pltpu.VMEM((half * FRAME, width), bf16),
            dma((8 + pairs,)),
            dma((3, pairs)),
            dma((3, pairs)),
            dma((3, half_pairs)),
            dma((3, half_pairs)),
            dma,
            dma,
            dma((7,)),
            dma((n_tm,)),
            dma((6,)),
            dma((6,)),
            dma((2,)),
            dma((2,)),
            dma,
            dma,
            dma((3,)),
            dma((3,)),
            dma((2, 3, max(7, 2 * reach))),
            dma((2, 3, n_tm)),
            dma((2, chunks)),
            dma((2, chunks)),
            dma((chunks,)),
            dma((chunks,)),
        ],
        compiler_params=pltpu.CompilerParams(
            collective_id=0, has_side_effects=True, vmem_limit_bytes=VMEM_LIMIT
        ),
    )(
        tokens.reshape(frames, FRAME, width), w_query, w_key, w_value, w_out,
        pool_kernel.transpose(1, 0, 2),
    )


def solution(mesh):
    shape = dict(mesh.shape)
    return jax.shard_map(
        functools.partial(per_device, shape["tm"], shape["chan"]),
        mesh=mesh,
        in_specs=(
            P("tm", "chan"),
            P(None, "chan"),
            P(None, "chan"),
            P(None, "chan"),
            P("chan", None),
            P(),
        ),
        out_specs=P("tm", "chan"),
        check_vma=False,
    )
```

```python
import functools

import jax
import jax.numpy as jnp
from jax import lax
from jax.experimental import pallas as pl
from jax.experimental.pallas import tpu as pltpu
from jax.sharding import PartitionSpec as P

D = 1024
HDIM = 64
HH = 16
WW = 16
FRAME = HH * WW
KEPT = 144
REST = FRAME - KEPT
CELLS = 16
CHUNK = 128
VMEM_LIMIT = 251 * 256 * 1024
EPSILON = 1e-06
MESH = pl.DeviceIdType.MESH
HIGHEST = lax.Precision.HIGHEST
f32 = jnp.float32
bf16 = jnp.bfloat16


def position(token):
    row, column = token >> 4, token & 15
    b, e = (row + 1) & 3, (column + 1) & 3
    i = jnp.where(b == 0, (row >> 2) + 1, row >> 2) & 3
    j = jnp.where(e == 0, (column >> 2) + 1, column >> 2) & 3
    rest = jnp.where(
        b == 3, KEPT + (row >> 2) * 16 + column, KEPT + 64 + (b * 4 + i) * 4 + (column >> 2)
    )
    return jnp.where((b == 3) | (e == 3), rest, (3 * b + e) * 16 + i * 4 + j)


def kernel(
    n_tm, reach, frames, width,
    tokens, w_query, w_key, w_value, w_out, pool_hbm, out,
    pool_kernel, raw, tok_a, tok_b, w_kv, wq_own, wq_far, wo, place, place_back, taps, pre,
    halo_out, halo_in, gat, k_big, v_big, queries, resid, early, att, leaving,
    local_sem, a_send, a_recv, b_send, b_recv, wqx_send, wqx_recv, wq_send, wq_recv,
    wox_send, wox_recv, wo_send, wo_recv, halo_send, halo_recv, kvx_send, kvx_recv,
    gat_send, gat_recv, att_send, att_recv, out_send, out_recv,
):
    tm = lax.axis_index("tm")
    me = lax.axis_index("chan")
    sib = me + 1 - 2 * lax.rem(me, 2)
    across = lax.rem(me + 2, 4)
    diag = lax.rem(sib + 2, 4)
    heads = width // HDIM
    spans = 2 * reach + 1
    pairs = frames // 2
    half = frames // 2
    half_pairs = half // 2
    first = lax.div(me, 2) * half
    other_first = half - first
    relayed = n_tm == 8
    parts = n_tm if relayed else 1
    part = tm if relayed else 0
    beside = tm + 1 - 2 * lax.rem(tm, 2)
    offsets = [-2, -1, 1, 2, 4] if relayed else [d for d in range(-reach, reach + 1) if d != 0]

    def tm_at(d):
        return lax.rem(tm + d + n_tm, n_tm)

    def columns(chan):
        return pl.ds(pl.multiple_of(chan * width, width), width)

    pair_order = [pairs - 1] + list(range(pairs - 1))
    raw_loads = {
        p: pltpu.make_async_copy(
            tokens.at[pl.ds(2 * p, 2)], raw.at[pl.ds(2 * p, 2)], local_sem.at[8 + p]
        )
        for p in pair_order
    }
    for p in pair_order:
        raw_loads[p].start()
    loads = [
        pltpu.make_async_copy(w_key, w_kv.at[:, pl.ds(0, width)], local_sem.at[0]),
        pltpu.make_async_copy(w_value, w_kv.at[:, pl.ds(width, width)], local_sem.at[1]),
        pltpu.make_async_copy(pool_hbm, pool_kernel, local_sem.at[2]),
        pltpu.make_async_copy(w_query, wq_own, local_sem.at[3]),
        pltpu.make_async_copy(
            w_out.at[:, columns(me)], wo.at[0, :, pl.ds(0, width)], local_sem.at[4]
        ),
        pltpu.make_async_copy(
            w_out.at[:, columns(across)], wo.at[0, :, pl.ds(width, width)], local_sem.at[5]
        ),
    ]
    for load in loads:
        load.start()

    barrier = pltpu.get_barrier_semaphore()
    for other in (sib, across, diag):
        pl.semaphore_signal(barrier, inc=1, device_id={"chan": other}, device_id_type=MESH)
    for d in offsets:
        pl.semaphore_signal(barrier, inc=1, device_id={"tm": tm_at(d)}, device_id_type=MESH)

    line = lax.broadcasted_iota(jnp.int32, (1, FRAME), 1)
    spot = lax.broadcasted_iota(jnp.int32, (FRAME, FRAME), 0)
    place[...] = jnp.where(position(line) == spot, 1.0, 0.0).astype(bf16)
    pl.semaphore_wait(barrier, 3 + len(offsets))

    sent = []

    def go(copy):
        copy.start()
        sent.append(copy)

    wq_rows = D // parts
    wo_parts = 2 if relayed else 1
    wo_part_at = lax.rem(tm, 2) if relayed else 0
    wo_rows = width // wo_parts

    def wq_part(index):
        return wq_far.at[pl.ds(pl.multiple_of(index * wq_rows, wq_rows), wq_rows)]

    def wo_half(slot, index):
        return wo.at[slot, pl.ds(pl.multiple_of(index * wo_rows, wo_rows), wo_rows)]

    wq_cross = pltpu.make_async_remote_copy(
        src_ref=w_query.at[pl.ds(pl.multiple_of(part * wq_rows, wq_rows), wq_rows)],
        dst_ref=wq_part(part), send_sem=wqx_send, recv_sem=wqx_recv,
        device_id={"chan": across}, device_id_type=MESH,
    )
    wq_cross.start()
    sent.append(wq_cross)

    def wo_copy(index, slot, other, block, chan):
        rows = (
            pl.ds(0, width)
            if slot == 1
            else pl.ds(pl.multiple_of(wo_part_at * wo_rows, wo_rows), wo_rows)
        )
        return pltpu.make_async_remote_copy(
            src_ref=w_out.at[rows, columns(chan)],
            dst_ref=wo.at[slot, rows, pl.ds(block * width, width)],
            send_sem=wox_send.at[index], recv_sem=wox_recv.at[index],
            device_id={"chan": other}, device_id_type=MESH,
        )

    wo_far = [
        wo_copy(0, 2, across, 0, across),
        wo_copy(1, 2, across, 1, me),
        wo_copy(2, 3, diag, 0, diag),
        wo_copy(3, 3, diag, 1, sib),
    ]
    wo_near = [wo_copy(4, 1, sib, 0, sib), wo_copy(5, 1, sib, 1, diag)]

    def gather(part_of, send_at, recv_at):
        def copy(index, source, target):
            ref = part_of(source)
            return pltpu.make_async_remote_copy(
                src_ref=ref, dst_ref=ref, send_sem=send_at(index), recv_sem=recv_at(source),
                device_id={"tm": target}, device_id_type=MESH,
            )

        def own(targets):
            for index, target in enumerate(targets):
                one = copy(index, tm, target)
                one.start()
                sent.append(one)

        def relay():
            for index, d in enumerate((2, 6, 4)):
                one = copy(4 + index, tm_at(d), beside)
                one.wait_recv()
                one.start()
                sent.append(one)

        def arrived(slot):
            copy(0, slot, beside).wait_recv()

        return own, relay, arrived

    wq_own_go, wq_relay, wq_arrived = gather(
        wq_part, lambda i: wq_send.at[i], lambda s: wq_recv.at[s]
    )

    def wo_swap(slot, index):
        ref = wo_half(slot, index)
        return pltpu.make_async_remote_copy(
            src_ref=ref, dst_ref=ref, send_sem=wo_send.at[slot - 2], recv_sem=wo_recv.at[slot - 2],
            device_id={"tm": beside}, device_id_type=MESH,
        )

    def wo_forward(slot):
        for copy in wo_far[2 * (slot - 2) : 2 * (slot - 1)]:
            copy.wait_recv()
        if relayed:
            go(wo_swap(slot, wo_part_at))

    plane = [tm_at(2), tm_at(6), tm_at(4), beside]
    from_beside = [beside] + [lax.rem(beside + d, n_tm) for d in (2, 6, 4)]

    def a_ref(slot, p):
        return tok_a.at[slot, pl.ds(2 * p, 2)]

    def b_ref(slot, base, p):
        return tok_b.at[slot, pl.ds(base + 2 * p, 2)]

    def chan_copy(ref, send, recv, other):
        return pltpu.make_async_remote_copy(
            src_ref=ref, dst_ref=ref, send_sem=send, recv_sem=recv,
            device_id={"chan": other}, device_id_type=MESH,
        )

    def a_copy(kind, p):
        slot = (me, me, across)[kind]
        return chan_copy(a_ref(slot, p), a_send.at[kind, p], a_recv.at[kind, p], (across, sib, sib)[kind])

    def a_arrival(kind, p):
        slot = (across, sib, diag)[kind]
        return chan_copy(a_ref(slot, p), a_send.at[kind, p], a_recv.at[kind, p], (across, sib, sib)[kind])

    def b_copy(kind, p):
        slot = (me, me, across)[kind]
        base = other_first if kind == 0 else first
        return chan_copy(
            b_ref(slot, base, p), b_send.at[kind, p], b_recv.at[kind, p], (across, sib, sib)[kind]
        )

    def b_arrival(kind, p):
        slot = (across, sib, diag)[kind]
        return chan_copy(
            b_ref(slot, first, p), b_send.at[kind, p], b_recv.at[kind, p], (across, sib, sib)[kind]
        )

    for p in pair_order:
        raw_loads[p].wait()
        for frame in (2 * p, 2 * p + 1):
            moved = jnp.dot(place[...], raw[frame], preferred_element_type=f32).astype(bf16)
            tok_a[me, frame] = moved[:KEPT]
            tok_b[me, frame] = moved[KEPT:]
        go(a_copy(0, p))
        go(a_copy(1, p))
    for copy in wo_near:
        go(copy)
    for p in range(half_pairs):
        go(b_copy(1, p))

    loads[2].wait()
    channel = lax.broadcasted_iota(jnp.int32, (HDIM, 2 * width), 1)
    inner = lax.broadcasted_iota(jnp.int32, (HDIM, 2 * width), 0)
    same = lax.rem(channel, HDIM) == inner
    spread_k = (same & (channel < width)).astype(f32)
    spread_v = (same & (channel >= width)).astype(f32)
    wide = jnp.dot(pool_kernel[:, 0], spread_k, precision=HIGHEST, preferred_element_type=f32)
    wide = wide + jnp.dot(pool_kernel[:, 1], spread_v, precision=HIGHEST, preferred_element_type=f32)
    cell = lax.broadcasted_iota(jnp.int32, (CELLS, 2 * width), 0)
    for tap in range(27):
        b, e = tap % 9 // 3, tap % 3
        value = jnp.broadcast_to(wide[tap : tap + 1], (CELLS, 2 * width))
        if b == 0:
            value = jnp.where(cell < 4, 0.0, value)
        if e == 0:
            value = jnp.where((cell & 3) == 0, 0.0, value)
        taps[tap] = value
    pre[...] = jnp.zeros_like(pre)
    line = lax.broadcasted_iota(jnp.int32, (FRAME, FRAME), 1)
    spot = lax.broadcasted_iota(jnp.int32, (FRAME, 1), 0)
    place_back[...] = jnp.where(position(spot) == line, 1.0, 0.0).astype(bf16)

    wq_cross.wait_recv()
    if relayed:
        wq_own_go(plane)

    halo = pltpu.make_async_remote_copy(
        src_ref=halo_out, dst_ref=halo_in, send_sem=halo_send, recv_sem=halo_recv,
        device_id={"tm": tm_at(1)}, device_id_type=MESH,
    )

    for load in loads[:2]:
        load.wait()

    def project(p, meanwhile=()):
        a_arrival(0, p).wait_recv()
        go(a_copy(2, p))
        def term(slot):
            return jnp.dot(
                tok_a[slot, 2 * p : 2 * p + 2].reshape(2 * KEPT, width),
                w_kv[pl.ds(pl.multiple_of(slot * width, width), width), :],
                preferred_element_type=f32,
            )

        total = term(me) + term(across)
        for step in meanwhile:
            step()
        a_arrival(1, p).wait_recv()
        total = total + term(sib)
        a_arrival(2, p).wait_recv()
        total = total + term(diag)
        field = total.astype(bf16).astype(f32)
        here, later = pre[p], None
        for tap in range(9):
            even = field[tap * CELLS : (tap + 1) * CELLS]
            odd = field[KEPT + tap * CELLS : KEPT + (tap + 1) * CELLS]
            here = here + even * taps[9 + tap] + odd * taps[18 + tap]
            ahead = odd * taps[tap]
            later = ahead if later is None else later + ahead
        pre[p] = here
        if p == pairs - 1:
            halo_out[...] = later
            go(halo)
        else:
            pre[p + 1] = pre[p + 1] + later

    g0 = lax.broadcasted_iota(jnp.int32, (width, width), 0) // HDIM
    g1 = lax.broadcasted_iota(jnp.int32, (width, width), 1) // HDIM
    averaging = jnp.where(g0 == g1, 1.0 / HDIM, 0.0).astype(bf16)
    phases = [(p, 1) for p in range(half_pairs)] + [(half_pairs, half_pairs)]

    def head_mean(x, pieces):
        stack, rest = [], x
        for _ in range(pieces):
            piece = rest.astype(bf16)
            stack.append(piece)
            rest = rest - piece.astype(f32)
        means = jnp.dot(jnp.concatenate(stack, axis=0), averaging, preferred_element_type=f32)
        total = None
        for index in reversed(range(pieces)):
            term = means[index * x.shape[0] : (index + 1) * x.shape[0]]
            total = term if total is None else total + term
        return total

    def normalise(phase):
        start, count = phases[phase]
        rows = count * CELLS
        pooled = pre[start : start + count].reshape(rows, 2 * width)
        if phase == 0:
            pooled = pooled + halo_in[...]
        x = jnp.concatenate([pooled[:, :width], pooled[:, width:]], axis=0)
        center = x - head_mean(x, 3)
        spread = head_mean(center * center, 2)
        result = (center * lax.rsqrt(spread + EPSILON)).astype(bf16)
        ours = gat.at[0, tm, pl.ds(start, count)]
        ours[:, :, :width] = result[:rows].reshape(count, CELLS, width)
        ours[:, :, width:] = result[rows:].reshape(count, CELLS, width)

    def block(g, slot, phase):
        return gat.at[g, slot, pl.ds(*phases[phase])]

    kv_gathers = {
        (g, phase): gather(
            lambda s, g=g, phase=phase: block(g, s, phase),
            lambda i, g=g, phase=phase: gat_send.at[g, phase, i],
            lambda s, g=g, phase=phase: gat_recv.at[g, phase, s],
        )
        for g in range(2)
        for phase in range(len(phases))
    }

    def kv_cross(phase):
        return pltpu.make_async_remote_copy(
            src_ref=block(0, tm, phase), dst_ref=block(1, tm, phase),
            send_sem=kvx_send.at[phase], recv_sem=kvx_recv.at[phase],
            device_id={"chan": across}, device_id_type=MESH,
        )

    kv_targets = plane if relayed else [tm_at(d) for d in offsets]

    def kv_send(phase):
        go(kv_cross(phase))
        kv_gathers[0, phase][0](kv_targets)

    def kv_forward(phase):
        kv_cross(phase).wait_recv()
        kv_gathers[1, phase][0](kv_targets)

    def kv_relay(g, phase):
        if relayed:
            kv_gathers[g, phase][1]()

    lane_head = lax.broadcasted_iota(jnp.int32, (CELLS, width), 1) // HDIM

    def spread_block(g, where, slot, phase):
        start, count = phases[phase]
        for pooled in range(start, start + count):
            at = (pooled * spans + where) * CELLS
            keys = gat[g, slot, pooled, :, :width]
            values = gat[g, slot, pooled, :, width:]
            for h in range(heads):
                k_big[g * heads + h, at : at + CELLS, :] = keys * jnp.where(
                    lane_head == h, HDIM**-0.5, 0.0
                ).astype(bf16)
                v_big[g * heads + h, at : at + CELLS, :] = values * jnp.where(
                    lane_head == h, 1.0, 0.0
                ).astype(bf16)

    def spread_blocks(g, phase):
        spread_block(g, 0, tm, phase)
        if relayed:
            for where, d in enumerate((2, 6)):
                spread_block(g, 1 + where, tm_at(d), phase)
            others, start = from_beside, 3
        else:
            others, start = [tm_at(d) for d in offsets], 1
        for where, slot in enumerate(others):
            kv_gathers[g, phase][2](slot)
            spread_block(g, start + where, slot, phase)

    def query_start(p):
        b_arrival(0, p).wait_recv()
        go(b_copy(2, p))

    def query(p):
        b_arrival(1, p).wait_recv()
        b_arrival(2, p).wait_recv()
        for local in (2 * p, 2 * p + 1):
            frame = first + local
            rows = slice(local * FRAME, (local + 1) * FRAME)
            near, far = None, None
            for s in range(4):
                block = jnp.concatenate([tok_a[s, frame], tok_b[s, frame]], axis=0)
                depth = slice(s * width, (s + 1) * width)
                near_term = jnp.dot(block, wq_own[depth], preferred_element_type=f32)
                far_term = jnp.dot(block, wq_far[depth], preferred_element_type=f32)
                near = near_term if near is None else near + near_term
                far = far_term if far is None else far + far_term
            back = place_back[...]
            queries[0, rows] = jnp.dot(back, near.astype(bf16), preferred_element_type=f32).astype(bf16)
            queries[1, rows] = jnp.dot(back, far.astype(bf16), preferred_element_type=f32).astype(bf16)
            block = jnp.concatenate([tok_a[across, frame], tok_b[across, frame]], axis=0)
            resid[rows] = jnp.dot(back, block, preferred_element_type=f32).astype(bf16)

    per_pair = 2 * FRAME // CHUNK
    phase_keys = spans * half_pairs * CELLS
    chunks = half * FRAME // CHUNK

    def rows_of(chunk):
        return pl.ds(pl.multiple_of(chunk * CHUNK, CHUNK), CHUNK)

    def att_copy(g, chunk):
        return pltpu.make_async_remote_copy(
            src_ref=att.at[2 * g, rows_of(chunk)], dst_ref=att.at[2 * g + 1, rows_of(chunk)],
            send_sem=att_send.at[g, chunk], recv_sem=att_recv.at[g, chunk],
            device_id={"chan": sib}, device_id_type=MESH,
        )

    def out_rows(base, chunk):
        return pl.ds(pl.multiple_of(base * FRAME + chunk * CHUNK, CHUNK), CHUNK)

    def out_copy(chunk, base):
        return pltpu.make_async_remote_copy(
            src_ref=leaving.at[rows_of(chunk)], dst_ref=out.at[out_rows(base, chunk)],
            send_sem=out_send.at[chunk], recv_sem=out_recv.at[chunk],
            device_id={"chan": across}, device_id_type=MESH,
        )

    def attend(rows, size, g, phase):
        q = queries[g, rows]
        head_of = lax.broadcasted_iota(jnp.int32, (size, width), 1) // HDIM
        keys = slice(phase * phase_keys, (phase + 1) * phase_keys)
        blended = top = divisor = None
        for h in range(heads):
            scores = lax.dot_general(
                q, k_big[g * heads + h, keys], (((1,), (1,)), ((), ())), preferred_element_type=f32
            )
            highest = jnp.max(scores, axis=-1, keepdims=True)
            weighted = jnp.exp(scores - highest)
            summed = jnp.sum(weighted, axis=-1, keepdims=True)
            term = jnp.dot(
                weighted.astype(bf16), v_big[g * heads + h, keys], preferred_element_type=f32
            )
            blended = term if blended is None else blended + term
            wide_top = jnp.broadcast_to(highest, (size, width))
            wide_sum = jnp.broadcast_to(summed, (size, width))
            top = wide_top if top is None else jnp.where(head_of == h, wide_top, top)
            divisor = wide_sum if divisor is None else jnp.where(head_of == h, wide_sum, divisor)
        return blended, top, divisor

    def attend_early(g, p):
        @pl.loop(2 * p, 2 * p + 2)
        def _(frame):
            rows = pl.ds(pl.multiple_of(frame * FRAME, FRAME), FRAME)
            early[0, g, rows], early[1, g, rows], early[2, g, rows] = attend(rows, FRAME, g, 0)

    def attend_late(chunk):
        rows = rows_of(chunk)
        for g in range(2):
            blended, top, divisor = attend(rows, CHUNK, g, 1)
            old_top = early[1, g, rows]
            new_top = jnp.maximum(top, old_top)
            keep, add = jnp.exp(old_top - new_top), jnp.exp(top - new_top)
            blended = early[0, g, rows] * keep + blended * add
            divisor = early[2, g, rows] * keep + divisor * add
            att[2 * g, rows] = (blended / divisor + queries[g, rows].astype(f32)).astype(bf16)
            att_copy(g, chunk).start()

    def finish(chunk):
        rows = rows_of(chunk)
        for g in range(2):
            att_copy(g, chunk).wait_recv()
        total = None
        for s in (0, 2, 1, 3):
            term = jnp.dot(att[s, rows], wo[s], preferred_element_type=f32)
            total = term if total is None else total + term
        leaving[rows] = (total[:, width:] + resid[rows].astype(f32)).astype(bf16)
        out_copy(chunk, first).start()
        per_frame = FRAME // CHUNK
        frame = first + lax.div(chunk, per_frame)
        inside = pl.ds(pl.multiple_of(lax.rem(chunk, per_frame) * CHUNK, CHUNK), CHUNK)
        out[out_rows(first, chunk)] = (total[:, :width] + raw[frame, inside].astype(f32)).astype(bf16)

    last = len(phases) - 1
    project(pair_order[0])
    project(pair_order[1])
    halo.wait_recv()
    normalise(0)
    kv_send(0)
    if relayed:
        wq_relay()
    project(pair_order[2])
    normalise(1)
    kv_send(1)
    go(b_copy(0, 0))
    kv_relay(0, 0)
    project(pair_order[3], [lambda: kv_forward(0), lambda: kv_forward(1)])
    normalise(2)
    kv_send(2)
    go(b_copy(0, 1))
    for copy in wo_far:
        go(copy)
    kv_relay(0, 1)
    query_start(0)
    kv_forward(2)
    kv_relay(1, 0)
    kv_relay(1, 1)
    loads[3].wait()
    if relayed:
        for slot in from_beside:
            wq_arrived(slot)
    query(0)
    spread_blocks(0, 0)
    spread_blocks(0, 1)
    kv_relay(0, 2)
    kv_relay(1, 2)
    attend_early(0, 0)
    wo_forward(2)
    query_start(1)
    spread_blocks(1, 0)
    spread_blocks(1, 1)
    attend_early(1, 0)
    query(1)
    wo_forward(3)
    attend_early(0, 1)
    attend_early(1, 1)
    spread_blocks(0, 2)
    spread_blocks(1, 2)
    for copy in wo_near:
        copy.wait_recv()
    for load in loads[4:]:
        load.wait()
    if relayed:
        for slot in (2, 3):
            wo_swap(slot, 1 - wo_part_at).wait_recv()

    attend_late(0)

    @pl.loop(1, chunks)
    def _(chunk):
        attend_late(chunk)
        finish(chunk - 1)

    finish(chunks - 1)

    @pl.loop(0, chunks)
    def _(chunk):
        for g in range(2):
            att_copy(g, chunk).wait_send()
        out_copy(chunk, other_first).wait_recv()
        out_copy(chunk, first).wait_send()

    for copy in sent:
        copy.wait_send()


def per_device(n_tm, n_chan, tokens, w_query, w_key, w_value, w_out, pool_kernel):
    rows, width = tokens.shape
    frames = rows // FRAME
    pairs = frames // 2
    half = frames // 2
    half_pairs = half // 2
    chunks = half * FRAME // CHUNK
    reach = min(6, (n_tm - 1) // 2)
    spans = 2 * reach + 1
    heads = width // HDIM
    block = pairs * CELLS
    dma = pltpu.SemaphoreType.DMA
    anywhere = pl.BlockSpec(memory_space=pltpu.HBM)
    vmem = pl.BlockSpec(memory_space=pltpu.VMEM)
    return pl.pallas_call(
        functools.partial(kernel, n_tm, reach, frames, width),
        out_shape=pltpu.VMEM((rows, width), bf16),
        in_specs=[anywhere] * 6,
        out_specs=vmem,
        scratch_shapes=[
            pltpu.VMEM((27, 2, HDIM), f32),
            pltpu.VMEM((frames, FRAME, width), bf16),
            pltpu.VMEM((n_chan, frames, KEPT, width), bf16),
            pltpu.VMEM((n_chan, frames, REST, width), bf16),
            pltpu.VMEM((D, 2 * width), bf16),
            pltpu.VMEM((D, width), bf16),
            pltpu.VMEM((D, width), bf16),
            pltpu.VMEM((n_chan, width, 2 * width), bf16),
            pltpu.VMEM((FRAME, FRAME), bf16),
            pltpu.VMEM((FRAME, FRAME), bf16),
            pltpu.VMEM((27, CELLS, 2 * width), f32),
            pltpu.VMEM((pairs, CELLS, 2 * width), f32),
            pltpu.VMEM((CELLS, 2 * width), f32),
            pltpu.VMEM((CELLS, 2 * width), f32),
            pltpu.VMEM((2, n_tm, pairs, CELLS, 2 * width), bf16),
            pltpu.VMEM((2 * heads, spans * block, width), bf16),
            pltpu.VMEM((2 * heads, spans * block, width), bf16),
            pltpu.VMEM((2, half * FRAME, width), bf16),
            pltpu.VMEM((half * FRAME, width), bf16),
            pltpu.VMEM((3, 2, half * FRAME, width), f32),
            pltpu.VMEM((n_chan, half * FRAME, width), bf16),
            pltpu.VMEM((half * FRAME, width), bf16),
            dma((8 + pairs,)),
            dma((3, pairs)),
            dma((3, pairs)),
            dma((3, half_pairs)),
            dma((3, half_pairs)),
            dma,
            dma,
            dma((7,)),
            dma((n_tm,)),
            dma((6,)),
            dma((6,)),
            dma((2,)),
            dma((2,)),
            dma,
            dma,
            dma((3,)),
            dma((3,)),
            dma((2, 3, max(7, 2 * reach))),
            dma((2, 3, n_tm)),
            dma((2, chunks)),
            dma((2, chunks)),
            dma((chunks,)),
            dma((chunks,)),
        ],
        compiler_params=pltpu.CompilerParams(
            collective_id=0, has_side_effects=True, vmem_limit_bytes=VMEM_LIMIT
        ),
    )(
        tokens.reshape(frames, FRAME, width), w_query, w_key, w_value, w_out,
        pool_kernel.transpose(1, 0, 2),
    )


def solution(mesh):
    shape = dict(mesh.shape)
    return jax.shard_map(
        functools.partial(per_device, shape["tm"], shape["chan"]),
        mesh=mesh,
        in_specs=(
            P("tm", "chan"),
            P(None, "chan"),
            P(None, "chan"),
            P(None, "chan"),
            P("chan", None),
            P(),
        ),
        out_specs=P("tm", "chan"),
        check_vma=False,
    )
```
